128 devices in a mesh: grp: 8 (over z, core), dev: 16 (over y, x).
Axes of the slice: x: 4, y: 4, z: 4, core: 2. Of those that a mesh axis runs over, the one named last changes fastest.
Arguments:
- a_blocks: bfloat16 [4096, 7, 192, 192], P(('grp', 'dev')), may hold values from -0.4375 to 0.4375
- prolong_t: bfloat16 [4096, 32, 192], P(('grp', 'dev')), may hold values from -1.796875 to 1.796875
- elem_slot: int32 [4096], P(('grp', 'dev')), may hold values from 0 to 5, as said below
- touch_agg: int32 [128, 6], replicated, may hold values from 0 to 527, as said below
- nbr: int32 [4096, 6], P(('grp', 'dev')), may hold values from -1 to 4095, as said below
- nbr_agg: int32 [4096, 6], P(('grp', 'dev')), may hold values from -1 to 527, as said below
- coarse_row: int32 [528], replicated, may hold values from 0 to 1407, as said below
Outputs:
- coarse: float32 [1408, 7, 1024], P('dev')
The draws below stay inside these ranges and needn't reach their ends.
Inputs may be any that keep to these rules, and one draw needn't show every extreme that they name: Element e lies on device e // 32 (devices numbered grp-major). elem_slot[e] is the position of e's aggregate in touch_agg[e // 32]. `touch_agg`: each row lists 6 distinct aggregates, exactly those of the device's elements; all devices that touch one aggregate share their grp index. `nbr`: global element index across each face, or -1 on the domain's boundary; adjacency is symmetric; a neighbour lies on the same device, or on the device whose grp index differs by one (same dev index), or whose dev index differs by one (same grp index); exactly 8 elements of a device have a neighbour on each existing device next along grp, and exactly 8 on each existing device next along dev. `nbr_agg`: the aggregate of the element nbr[e, f], -1 exactly where nbr[e, f] is -1. Distinct values; aggregate a's row belongs to dev index coarse_row[a] // 88. Of the aggregates touched by one device at most 1 belong to one dev index, and of those touched by the devices of one grp index at most 11; one dev index reaches both bounds and holds 88 rows.
All inputs are finite; a program needn't handle non-finite values.
Results may differ from the reference program's by a relative error of at most 0.005.
Values may be sent and summed in bfloat16 or wider, within the bound.
No kernel may reach another device: no remote copies, remote signals or barrier semaphores. Data moves between devices by JAX's collectives and lax.ppermute only.
A program may use at most 128 MiB of HBM per device.

```python
import jax
import jax.numpy as jnp
from jax import lax

B = 192
C = 32
EX = 4
EY = 4
EZ = 2
E_DEV = 32
ELEMS = 4096
TOUCH = 6
SEND_CAP = 1
NYBOX = 33
AGG = 528
ROWS_OWN = 88
COARSE = 1408
N_GRP = 8
N_DEV = 16


def face_fields(field):
    padded = jnp.pad(field, 1, constant_values=-1)
    return jnp.stack([padded[:-2, 1:-1, 1:-1], padded[2:, 1:-1, 1:-1], padded[1:-1, :-2, 1:-1], padded[1:-1, 2:, 1:-1], padded[1:-1, 1:-1, :-2], padded[1:-1, 1:-1, 2:]], axis=-1)


def geometry(key):
    keys = jax.random.split(jax.random.fold_in(key, 11), 6)
    devices = N_GRP * N_DEV
    half_x = EX // 2
    half_y = EY // 2
    span_y = half_y + 1
    half_z = EZ // 2
    coord_x, coord_y, coord_z = jnp.meshgrid(jnp.arange(N_GRP * EX, dtype=jnp.int32), jnp.arange(N_DEV * EY, dtype=jnp.int32), jnp.arange(EZ, dtype=jnp.int32), indexing='ij')
    grp_of = coord_x // EX
    dev_of = coord_y // EY
    device = grp_of * N_DEV + dev_of
    canon = (coord_x % EX * EY + coord_y % EY) * EZ + coord_z
    local_perms = jax.vmap(lambda k: jax.random.permutation(k, E_DEV))(jax.random.split(keys[0], devices))
    global_id = (device * E_DEV + local_perms[device, canon]).astype(jnp.int32)
    box_x = coord_x // 2
    box_y = (coord_y + 1) // 2
    box_z = coord_z // 2
    box = (box_x * NYBOX + box_y) * half_z + box_z
    box_perm = jax.random.permutation(keys[1], AGG).astype(jnp.int32)
    agg = box_perm[box]
    canon_touch = ((box_x - grp_of * half_x) * span_y + (box_y - dev_of * half_y)) * half_z + box_z
    touch_perms = jax.vmap(lambda k: jax.random.permutation(k, TOUCH))(jax.random.split(keys[2], devices))
    slot = touch_perms[device, canon_touch].astype(jnp.int32)
    touch = jnp.zeros((devices, TOUCH), jnp.int32).at[device, slot].set(agg)
    classes = jnp.arange(TOUCH, dtype=jnp.int32)
    class_ry = classes // half_z % span_y
    shuffled = jax.random.permutation(keys[3], TOUCH).astype(jnp.int32)
    score = jnp.where(class_ry != 0, TOUCH, 0) + shuffled
    order = jnp.argsort(score, stable=True)
    class_rank = jnp.zeros((TOUCH,), jnp.int32).at[order].set(classes)
    owner_perm = jax.random.permutation(keys[4], N_DEV).astype(jnp.int32)
    owner_class = jnp.where(class_rank < SEND_CAP, owner_perm[0], owner_perm[1 + (class_rank - SEND_CAP) % (N_DEV - 1)])
    grid_x, grid_y, grid_z = jnp.meshgrid(jnp.arange(N_GRP * half_x, dtype=jnp.int32), jnp.arange(NYBOX, dtype=jnp.int32), jnp.arange(half_z, dtype=jnp.int32), indexing='ij')
    class_box = ((grid_x % half_x * span_y + grid_y % span_y) * half_z + grid_z).reshape(-1)
    owner_box = owner_class[class_box]
    priority = jax.random.permutation(keys[5], AGG).astype(jnp.int32)
    earlier = (owner_box[None, :] == owner_box[:, None]) & (priority[None, :] < priority[:, None])
    position = jnp.sum(earlier.astype(jnp.int32), axis=1)
    row_box = (owner_box * ROWS_OWN + position).astype(jnp.int32)
    coarse_rows = jnp.zeros((AGG,), jnp.int32).at[box_perm].set(row_box)
    flat_ids = global_id.reshape(-1)
    elem_slots = jnp.zeros((ELEMS,), jnp.int32).at[flat_ids].set(slot.reshape(-1))
    neighbours = jnp.zeros((ELEMS, 6), jnp.int32).at[flat_ids].set(face_fields(global_id).reshape(-1, 6))
    neighbour_aggs = jnp.zeros((ELEMS, 6), jnp.int32).at[flat_ids].set(face_fields(agg).reshape(-1, 6))
    return (elem_slots, touch, neighbours, neighbour_aggs, coarse_rows)


def draw_elem_slot(key, part):
    return geometry(key)[0]


def draw_touch_agg(key, part):
    return geometry(key)[1]


def draw_nbr(key, part):
    return geometry(key)[2]


def draw_nbr_agg(key, part):
    return geometry(key)[3]


def draw_coarse_row(key, part):
    return geometry(key)[4]


def level_of(rng, shape, cuts, smallest, top_value):
    gain, own = 1.0, jax.random.fold_in(rng, 6)
    for axis_at, blocks in cuts:
        steps = jnp.exp(jax.random.uniform(jax.random.fold_in(own, axis_at), (blocks,), jnp.float32, smallest / len(cuts), top_value / len(cuts)))
        gain = gain * jnp.repeat(steps, shape[axis_at] // blocks).reshape([-1 if axis == axis_at else 1 for axis in range(len(shape))])
    return gain


def centred(stream_key, dims, scale, bound, shards=(), kind=jnp.bfloat16):
    result = jax.random.normal(stream_key, dims, jnp.float32) * scale
    if len(shards) > 0:
        result = level_of(stream_key, dims, shards, -0.22, 0.18) * result
    return jnp.clip(result, min=-bound, max=bound).astype(kind)


def setup_inputs(seed: int = 0) -> dict:
    streams_of = jax.random.split(jax.random.key(seed), 8)
    a_blocks = centred(streams_of[0], (ELEMS, 7, B, B), B ** -0.5, 0.4375, ((0, 128),))
    prolong_t = centred(streams_of[1], (ELEMS, C, B), 0.3, 1.796875, ((0, 128),))
    elem_slot = draw_elem_slot(jax.random.fold_in(streams_of[7], 71), 0)
    touch_agg = draw_touch_agg(jax.random.fold_in(streams_of[7], 71), 0)
    nbr = draw_nbr(jax.random.fold_in(streams_of[7], 71), 0)
    nbr_agg = draw_nbr_agg(jax.random.fold_in(streams_of[7], 71), 0)
    coarse_row = draw_coarse_row(jax.random.fold_in(streams_of[7], 71), 0)
    return dict(a_blocks=a_blocks, prolong_t=prolong_t, elem_slot=elem_slot, touch_agg=touch_agg, nbr=nbr, nbr_agg=nbr_agg, coarse_row=coarse_row)


def reference(a_blocks, prolong_t, elem_slot, touch_agg, nbr, nbr_agg, coarse_row):
    elems = a_blocks.shape[0]
    devices = elems // E_DEV
    owner_device = (jnp.arange(elems, dtype=jnp.int32) // E_DEV).astype(jnp.int32)
    agg_of = touch_agg[owner_device, elem_slot]
    valid = nbr >= 0
    safe_nbr = jnp.where(valid, nbr, 0).astype(jnp.int32)

    def per_device(index):
        start = (index * E_DEV).astype(jnp.int32)
        blocks = lax.dynamic_slice_in_dim(a_blocks, start, E_DEV, 0).astype(jnp.float32)
        left = lax.dynamic_slice_in_dim(prolong_t, start, E_DEV, 0)
        left_blocks = jnp.einsum("ecb,ekbd->ekcd", left.astype(jnp.float32), blocks,
                                 precision=lax.Precision.HIGHEST).astype(jnp.bfloat16)
        across = lax.dynamic_slice_in_dim(safe_nbr, start, E_DEV, 0)
        right = jnp.concatenate([left[:, None], prolong_t[across]], axis=1)
        products = jnp.einsum("ekcd,ekxd->ekcx", left_blocks.astype(jnp.float32), right.astype(jnp.float32),
                              precision=lax.Precision.HIGHEST)
        return products.reshape(E_DEV, 7, C * C)

    products = lax.map(per_device, jnp.arange(devices, dtype=jnp.int32)).reshape(elems, 7, C * C)
    same = valid & (nbr_agg == agg_of[:, None])
    apart = valid & jnp.logical_not(same)
    faces = products[:, 1:]
    diagonal = products[:, 0] + jnp.sum(jnp.where(same[:, :, None], faces, jnp.float32(0.0)), axis=1)
    contrib = jnp.concatenate([diagonal[:, None], jnp.where(apart[:, :, None], faces, jnp.float32(0.0))], axis=1)
    coarse_sum = jax.ops.segment_sum(contrib, agg_of, num_segments=AGG)
    coarse = jnp.zeros((COARSE, 7, C * C), jnp.float32).at[coarse_row].set(coarse_sum)
    return coarse
```

```python
import jax
import jax.numpy as jnp
from jax import lax
from jax.experimental import pallas as pl
from jax.experimental.pallas import tpu as pltpu
from jax.sharding import PartitionSpec as P

TOUCH = 6
FACES = 6
BLOCKS = 7
LANES = 128
HALO = 8
F32 = jnp.float32
BF16 = jnp.bfloat16
SMEM = pltpu.MemorySpace.SMEM
VMEM = pltpu.MemorySpace.VMEM


def position(n_dev):
    return lax.axis_index("grp") * n_dev + lax.axis_index("dev")


def pack_kernel(n_dev, nbr_ref, p_ref, *refs):
    outs, bufs = refs[:4], refs[4:]
    e_dev = p_ref.shape[0]
    shift = e_dev.bit_length() - 1
    device = position(n_dev)
    homes = (device - n_dev, device + n_dev, device - 1, device + 1)

    def step(e, counts):
        hits = [jnp.bool_(False)] * 4
        for f in range(FACES):
            home = lax.shift_right_arithmetic(nbr_ref[e, f], shift)
            hits = [hit | (home == h) for hit, h in zip(hits, homes)]
        block = p_ref[e]
        new = []
        for d in range(4):
            bufs[d][jnp.minimum(counts[d], HALO)] = block
            new.append(counts[d] + hits[d].astype(jnp.int32))
        return tuple(new)

    lax.fori_loop(0, e_dev, step, (jnp.int32(0),) * 4, unroll=4)
    for d in range(4):
        outs[d][...] = bufs[d][0:HALO]


def main_kernel(n_dev, rows_own, slot_ref, nbr_ref, nagg_ref, crow_ref, touch_hbm, a_hbm, p_ref, h0, h1, h2, h3,
                out_ref, abuf, pool, acc, touch, seen, place, a_sems, t_sem):
    e_dev, width_c, _ = p_ref.shape
    shift = e_dev.bit_length() - 1
    device = position(n_dev)
    base8 = pl.multiple_of((device // 8) * 8, 8)
    row8 = device % 8
    t_copy = pltpu.make_async_copy(touch_hbm.at[pl.ds(base8, 8)], touch, t_sem)
    t_copy.start()

    def fetch(e):
        return pltpu.make_async_copy(a_hbm.at[e], abuf.at[e], a_sems.at[e])

    for e in range(e_dev):
        fetch(e).start()
    acc[...] = jnp.zeros_like(acc)
    out_ref[...] = jnp.zeros_like(out_ref)
    pool[0:e_dev] = p_ref[...]
    for d, h in enumerate((h0, h1, h2, h3)):
        pool[e_dev + HALO * d : e_dev + HALO * (d + 1)] = h[...]
    t_copy.wait()

    def clear(i, c):
        seen[i] = 0
        return c

    lax.fori_loop(0, 5 * e_dev, clear, 0, unroll=8)
    homes = (device - n_dev, device + n_dev, device - 1, device + 1)

    def side_of(n):
        home = lax.shift_right_arithmetic(n, shift)
        side = jnp.int32(4)
        for d, h in enumerate(homes):
            side = jnp.where(home == h, d, side)
        return side

    def mark(e, c):
        for f in range(FACES):
            n = nbr_ref[e, f]
            seen[side_of(n) * e_dev + (n & (e_dev - 1))] = 1
        return c

    lax.fori_loop(0, e_dev, mark, 0, unroll=2)

    def order(i, counts):
        new = []
        for d in range(4):
            at = d * e_dev + i
            hit = seen[at]
            place[at] = e_dev + HALO * d + jnp.minimum(counts[d], HALO - 1)
            new.append(counts[d] + hit)
        place[4 * e_dev + i] = i
        return tuple(new)

    lax.fori_loop(0, e_dev, order, (jnp.int32(0),) * 4, unroll=2)

    def element(e, c):
        fetch(e).wait()
        left = p_ref[e]
        slot = slot_ref[e]
        own = touch[row8, slot]
        total = None
        for k in range(BLOCKS):
            lk = jnp.dot(left, abuf[e, k], preferred_element_type=F32).astype(BF16)
            if k == 0:
                right = left
            else:
                n = nbr_ref[e, k - 1]
                right = pool[place[side_of(n) * e_dev + (n & (e_dev - 1))]]
            prod = lax.dot_general(lk, right, (((1,), (1,)), ((), ())), preferred_element_type=F32)
            if k == 0:
                total = prod
                continue
            valid = n >= 0
            same = valid & (nagg_ref[e, k - 1] == own)
            apart = valid & jnp.logical_not(nagg_ref[e, k - 1] == own)
            total = total + jnp.where(same, prod, 0.0)
            at = pl.multiple_of((slot * 8 + k) * width_c, width_c)
            acc[pl.ds(at, width_c), 0:width_c] += jnp.where(apart, prod, 0.0)
        at = pl.multiple_of(slot * 8 * width_c, width_c)
        acc[pl.ds(at, width_c), 0:width_c] += total
        return c

    lax.fori_loop(0, e_dev, element, 0)

    lane = lax.broadcasted_iota(jnp.int32, (8, LANES), 1)
    sub = lax.broadcasted_iota(jnp.int32, (8, LANES), 0)
    per = LANES // width_c
    for t in range(TOUCH):
        row = crow_ref[touch[row8, t]]
        owner = row // rows_own
        code = (row - owner * rows_own + 1).astype(F32)
        for j in range(width_c // per):
            value = None
            for i in range(per):
                piece = acc[pl.ds(t * 8 * width_c + j * per + i, 8, stride=width_c), :]
                if i == 0:
                    value = piece
                else:
                    piece = pltpu.roll(piece, i * width_c, 1)
                    value = jnp.where(lane >= i * width_c, piece, value)
            value = jnp.where(sub == 7, code, value)
            out_ref[owner, :, j * LANES : (j + 1) * LANES] = value.astype(BF16)


def combine_kernel(rows_own, in_ref, out_ref, sums, rank, codes):
    n_dev, _, width = in_ref.shape
    group_rows = out_ref.shape[0]

    def clear(i, c):
        rank[i] = -1
        return c

    lax.fori_loop(0, rows_own + 1, clear, 0, unroll=8)
    for r in range(group_rows + 1):
        codes[r] = 0
    sums[...] = jnp.zeros_like(sums)
    used = jnp.int32(0)
    for d in range(n_dev):
        code = in_ref[d, :, 0:LANES].astype(F32)[7, 0].astype(jnp.int32)
        old = rank[code]
        fresh = (code > 0) & (old < 0)
        at = jnp.where(code > 0, jnp.where(old < 0, jnp.minimum(used, group_rows - 1), old), group_rows)
        rank[code] = jnp.where(code > 0, at, -1)
        codes[at] = code
        used = used + fresh.astype(jnp.int32)
        sums[at] += in_ref[d].astype(F32)
    sub = lax.broadcasted_iota(jnp.int32, (8, width), 0)
    for r in range(group_rows):
        out_ref[r] = jnp.where(sub == 7, codes[r].astype(F32), sums[r]).astype(BF16)


def scatter_kernel(*refs):
    ins, out_ref, sink = refs[:-2], refs[-2], refs[-1]
    rows = out_ref.shape[0]
    out_ref[...] = jnp.zeros_like(out_ref)

    def put(block):
        value = block.astype(F32)
        code = value[7, 0].astype(jnp.int32)

        @pl.when(code > 0)
        def _():
            out_ref[jnp.clip(code - 1, 0, rows - 1)] = value[0:7]

    for ref in ins:
        if len(ref.shape) == 3:
            for r in range(ref.shape[0]):
                put(ref[r])
        else:
            for q in range(ref.shape[0]):
                for r in range(ref.shape[1]):
                    put(ref[q, r])


def on_device(a_blocks, prolong_t, elem_slot, touch_agg, nbr, nbr_agg, coarse_row):
    n_grp = lax.axis_size("grp")
    n_dev = lax.axis_size("dev")
    e_dev, width_c, width_b = prolong_t.shape
    half = 2
    group_rows = ((n_dev * half + 1) + half) // (half + 1)
    rows_own = n_grp * group_rows
    width = width_c * width_c
    smem = pl.BlockSpec(memory_space=SMEM)
    vmem = pl.BlockSpec(memory_space=VMEM)
    hbm = pl.BlockSpec(memory_space=pl.ANY)
    params = pltpu.CompilerParams(vmem_limit_bytes=56 << 20)

    def pack(*args):
        return pack_kernel(n_dev, *args)

    halo_shape = jax.ShapeDtypeStruct((HALO, width_c, width_b), BF16)
    packed = pl.pallas_call(
        pack, out_shape=(halo_shape,) * 4, in_specs=[smem, vmem], out_specs=(vmem,) * 4,
        scratch_shapes=[pltpu.VMEM((HALO + 1, width_c, width_b), BF16)] * 4, compiler_params=params, name="pack",
    )(nbr, prolong_t)
    up = lambda size: [(i, i + 1) for i in range(size - 1)]
    down = lambda size: [(i + 1, i) for i in range(size - 1)]
    from_low = lax.ppermute(packed[1], "grp", up(n_grp))
    from_high = lax.ppermute(packed[0], "grp", down(n_grp))
    from_left = lax.ppermute(packed[3], "dev", up(n_dev))
    from_right = lax.ppermute(packed[2], "dev", down(n_dev))

    def main(*args):
        return main_kernel(n_dev, rows_own, *args)

    outgoing = pl.pallas_call(
        main, out_shape=jax.ShapeDtypeStruct((n_dev, 8, width), BF16),
        in_specs=[smem] * 4 + [hbm] * 2 + [vmem] * 5, out_specs=vmem,
        scratch_shapes=[
            pltpu.VMEM((e_dev, BLOCKS, width_b, width_b), BF16),
            pltpu.VMEM((e_dev + 4 * HALO, width_c, width_b), BF16),
            pltpu.VMEM((TOUCH * 8 * width_c, LANES), F32),
            pltpu.SMEM((8, TOUCH), jnp.int32),
            pltpu.SMEM((5 * e_dev,), jnp.int32),
            pltpu.SMEM((5 * e_dev,), jnp.int32),
            pltpu.SemaphoreType.DMA((e_dev,)),
            pltpu.SemaphoreType.DMA(()),
        ],
        compiler_params=params, name="products",
    )(elem_slot, nbr, nbr_agg, coarse_row, touch_agg, a_blocks, prolong_t, from_low, from_high, from_left, from_right)
    incoming = lax.all_to_all(outgoing, "dev", split_axis=0, concat_axis=0, tiled=True)

    def combine(*args):
        return combine_kernel(rows_own, *args)

    mine = pl.pallas_call(
        combine, out_shape=jax.ShapeDtypeStruct((group_rows, 8, width), BF16), in_specs=[vmem], out_specs=vmem,
        scratch_shapes=[pltpu.VMEM((group_rows + 1, 8, width), F32), pltpu.SMEM((rows_own + 1,), jnp.int32),
                        pltpu.SMEM((group_rows + 1,), jnp.int32)],
        compiler_params=params, name="combine",
    )(incoming)
    swap = [(i, i ^ 1) for i in range(n_grp)]
    across = [lax.ppermute(mine, "grp", [(i, (i + 2 * k) % n_grp) for i in range(n_grp)]) for k in range(1, n_grp // 2)]
    twin = lax.ppermute(mine, "grp", swap)
    others = lax.ppermute(jnp.stack(across), "grp", swap)
    pieces = (mine, twin, *across, others)
    return pl.pallas_call(
        scatter_kernel, out_shape=jax.ShapeDtypeStruct((rows_own, BLOCKS, width), F32), in_specs=[vmem] * len(pieces),
        out_specs=vmem, scratch_shapes=[pltpu.SMEM((1,), jnp.int32)], compiler_params=params, name="scatter",
    )(*pieces)


def solution(mesh):
    in_specs = (
        P(("grp", "dev"), None, None, None),
        P(("grp", "dev"), None, None),
        P(("grp", "dev")),
        P(),
        P(("grp", "dev"), None),
        P(("grp", "dev"), None),
        P(),
    )
    return jax.shard_map(
        on_device, mesh=mesh, in_specs=in_specs, out_specs=P("dev", None, None), check_vma=False
    )
```

```python
import jax
import jax.numpy as jnp
from jax import lax
from jax.experimental import pallas as pl
from jax.experimental.pallas import tpu as pltpu
from jax.sharding import PartitionSpec as P

TOUCH = 6
FACES = 6
BLOCKS = 7
LANES = 128
HALO = 8
F32 = jnp.float32
BF16 = jnp.bfloat16
SMEM = pltpu.MemorySpace.SMEM
VMEM = pltpu.MemorySpace.VMEM


def position(n_dev):
    return lax.axis_index("grp") * n_dev + lax.axis_index("dev")


def pack_kernel(n_dev, nbr_ref, p_ref, *refs):
    outs, bufs = refs[:4], refs[4:]
    e_dev = p_ref.shape[0]
    shift = e_dev.bit_length() - 1
    device = position(n_dev)
    homes = (device - n_dev, device + n_dev, device - 1, device + 1)

    def step(e, counts):
        hits = [jnp.bool_(False)] * 4
        for f in range(FACES):
            home = lax.shift_right_arithmetic(nbr_ref[f, e], shift)
            hits = [hit | (home == h) for hit, h in zip(hits, homes)]
        block = p_ref[e]
        new = []
        for d in range(4):
            bufs[d][jnp.minimum(counts[d], HALO)] = block
            new.append(counts[d] + hits[d].astype(jnp.int32))
        return tuple(new)

    lax.fori_loop(0, e_dev, step, (jnp.int32(0),) * 4, unroll=4)
    for d in range(4):
        outs[d][...] = bufs[d][0:HALO]


def main_kernel(n_dev, rows_own, slot_ref, nbr_ref, nagg_ref, crow_ref, touch_ref, a_hbm, p_ref, h0, h1, h2, h3,
                out_ref, abuf, pool, acc, lefts0, lefts1, seen, place, a_sems, h_sems):
    e_dev, width_c, _ = p_ref.shape
    shift = e_dev.bit_length() - 1
    device = position(n_dev)

    def fetch(e):
        return pltpu.make_async_copy(a_hbm.at[e], abuf.at[e], a_sems.at[e])

    for e in range(e_dev):
        fetch(e).start()
    halos = [
        pltpu.make_async_copy(h, pool.at[pl.ds(e_dev + HALO * d, HALO)], h_sems.at[d])
        for d, h in enumerate((h0, h1, h2, h3))
    ]
    for copy in halos:
        copy.start()
    acc[...] = jnp.zeros_like(acc)
    out_ref[...] = jnp.zeros_like(out_ref)
    pool[0:e_dev] = p_ref[...]

    def clear(i, c):
        seen[i] = 0
        return c

    lax.fori_loop(0, 5 * e_dev, clear, 0, unroll=8)
    homes = (device - n_dev, device + n_dev, device - 1, device + 1)

    def side_of(n):
        home = lax.shift_right_arithmetic(n, shift)
        side = jnp.int32(4)
        for d, h in enumerate(homes):
            side = jnp.where(home == h, d, side)
        return side

    def mark(e, c):
        for f in range(FACES):
            n = nbr_ref[f, e]
            seen[side_of(n) * e_dev + (n & (e_dev - 1))] = 1
        return c

    lax.fori_loop(0, e_dev, mark, 0, unroll=2)

    def order(i, counts):
        new = []
        for d in range(4):
            at = d * e_dev + i
            hit = seen[at]
            place[at] = e_dev + HALO * d + jnp.minimum(counts[d], HALO - 1)
            new.append(counts[d] + hit)
        place[4 * e_dev + i] = i
        return tuple(new)

    lax.fori_loop(0, e_dev, order, (jnp.int32(0),) * 4, unroll=2)
    for copy in halos:
        copy.wait()

    def make_lefts(e, lefts):
        left = p_ref[e]
        for k in range(BLOCKS):
            lefts[k] = jnp.dot(left, abuf[e, k], preferred_element_type=F32).astype(BF16)

    def add_products(e, lefts):
        slot = slot_ref[e]
        own = touch_ref[slot, device]
        total = None
        for k in range(BLOCKS):
            if k == 0:
                right = p_ref[e]
            else:
                n = nbr_ref[k - 1, e]
                right = pool[place[side_of(n) * e_dev + (n & (e_dev - 1))]]
            prod = lax.dot_general(lefts[k], right, (((1,), (1,)), ((), ())), preferred_element_type=F32)
            if k == 0:
                total = prod
                continue
            valid = n >= 0
            same = valid & (nagg_ref[k - 1, e] == own)
            apart = valid & (nagg_ref[k - 1, e] != own)
            total = total + jnp.where(same, prod, 0.0)
            at = pl.multiple_of((slot * 8 + k) * width_c, width_c)
            acc[pl.ds(at, width_c), 0:width_c] += jnp.where(apart, prod, 0.0)
        at = pl.multiple_of(slot * 8 * width_c, width_c)
        acc[pl.ds(at, width_c), 0:width_c] += total

    fetch(0).wait()
    make_lefts(0, lefts0)

    def two(i, c):
        e = 2 * i + 1
        fetch(e).wait()
        fetch(e + 1).wait()
        add_products(e - 1, lefts0)
        make_lefts(e, lefts1)
        add_products(e, lefts1)
        make_lefts(e + 1, lefts0)
        return c

    lax.fori_loop(0, e_dev // 2 - 1, two, 0)
    fetch(e_dev - 1).wait()
    make_lefts(e_dev - 1, lefts1)
    add_products(e_dev - 2, lefts0)
    add_products(e_dev - 1, lefts1)

    lane = lax.broadcasted_iota(jnp.int32, (8, LANES), 1)
    sub = lax.broadcasted_iota(jnp.int32, (8, LANES), 0)
    per = LANES // width_c
    for t in range(TOUCH):
        row = crow_ref[touch_ref[t, device]]
        owner = row // rows_own
        code = (row - owner * rows_own + 1).astype(F32)
        for j in range(width_c // per):
            value = None
            for i in range(per):
                piece = acc[pl.ds(t * 8 * width_c + j * per + i, 8, stride=width_c), :]
                if i == 0:
                    value = piece
                else:
                    piece = pltpu.roll(piece, i * width_c, 1)
                    value = jnp.where(lane >= i * width_c, piece, value)
            value = jnp.where(sub == 7, code, value)
            out_ref[owner, :, j * LANES : (j + 1) * LANES] = value.astype(BF16)


def combine_kernel(rows_own, group_rows, in_ref, out_ref, rank, codes):
    slots, width = in_ref.shape
    n_dev = slots // 8
    piece = out_ref.shape[0]

    def clear(i, c):
        rank[i] = -1
        return c

    lax.fori_loop(0, rows_own + 1, clear, 0, unroll=8)
    for r in range(group_rows + 1):
        codes[r] = 0
    used = jnp.int32(0)
    lane = lax.broadcasted_iota(jnp.int32, (1, slots), 1)
    key = jnp.full((1, slots), -1, jnp.int32)
    for d in range(n_dev):
        code = in_ref[8 * d : 8 * d + 8, 0:LANES].astype(F32)[7, 0].astype(jnp.int32)
        old = rank[code]
        fresh = (code > 0) & (old < 0)
        at = jnp.where(code > 0, jnp.where(old < 0, jnp.minimum(used, group_rows - 1), old), group_rows)
        rank[code] = jnp.where(code > 0, at, -1)
        codes[at] = code
        used = used + fresh.astype(jnp.int32)
        mine = (lane >= 8 * d) & (lane < 8 * d + 7)
        key = jnp.where(mine, jnp.where(code > 0, (lane - 8 * d) * group_rows + at, -1), key)
    row = lax.broadcasted_iota(jnp.int32, (piece, slots), 0)
    chosen = jnp.where(row == key, 1.0, 0.0).astype(BF16)
    out = jnp.dot(chosen, in_ref[...], preferred_element_type=F32)
    at = lax.broadcasted_iota(jnp.int32, (1, width), 1) % piece
    of_row = at % group_rows
    tags = jnp.zeros((1, width), F32)
    for r in range(group_rows):
        tags = jnp.where((of_row == r) & (at < BLOCKS * group_rows), codes[r].astype(F32), tags)
    rows = lax.broadcasted_iota(jnp.int32, (piece, width), 0)
    out_ref[...] = jnp.where(rows >= BLOCKS * group_rows, tags, out).astype(BF16)


def scatter_kernel(rows_own, group_rows, *refs):
    ins, out_hbm, held, chosen, out_buf, in_sems, out_sems = refs[:-6], *refs[-6:]
    total, width = out_buf.shape
    piece = ins[0].shape[-2]
    sources = [ref if len(ref.shape) == 2 else ref.at[q] for ref in ins for q in range(1 if len(ref.shape) == 2 else ref.shape[0])]
    copies = [
        pltpu.make_async_copy(ref, held.at[pl.ds(q * piece, piece)], in_sems.at[q]) for q, ref in enumerate(sources)
    ]
    for copy in copies:
        copy.start()
    depth = held.shape[0]
    lane = lax.broadcasted_iota(jnp.int32, (1, depth), 1)
    in_piece = lane % piece
    block = in_piece // group_rows
    for copy in copies:
        copy.wait()
    tags = jnp.zeros((1, depth), F32)
    for q in range(len(sources)):
        tag = held[(q + 1) * piece - 8 : (q + 1) * piece, 0:depth].astype(F32)[7:8]
        tags = jnp.where((lane >= q * piece) & (lane < (q + 1) * piece), tag, tags)
    tags = tags.astype(jnp.int32)
    key = jnp.where((tags > 0) & (block < BLOCKS), block * rows_own + tags - 1, -1)
    for s in range(BLOCKS):
        row = lax.broadcasted_iota(jnp.int32, (rows_own, depth), 0) + s * rows_own
        chosen[s * rows_own : (s + 1) * rows_own] = jnp.where(row == key, 1.0, 0.0).astype(BF16)
    n_out = out_sems.shape[0]
    step = width // n_out
    outs = []
    for n in range(n_out):
        cols = pl.ds(n * step, step)
        out_buf[:, n * step : (n + 1) * step] = jnp.dot(
            chosen[...], held[:, n * step : (n + 1) * step], preferred_element_type=F32
        )
        copy = pltpu.make_async_copy(out_buf.at[:, cols], out_hbm.at[:, cols], out_sems.at[n])
        copy.start()
        outs.append(copy)
    for copy in outs:
        copy.wait()


def on_device(a_blocks, prolong_t, elem_slot, touch_agg, nbr, nbr_agg, coarse_row):
    n_grp = lax.axis_size("grp")
    n_dev = lax.axis_size("dev")
    e_dev, width_c, width_b = prolong_t.shape
    half = 2
    group_rows = ((n_dev * half + 1) + half) // (half + 1)
    rows_own = n_grp * group_rows
    width = width_c * width_c
    smem = pl.BlockSpec(memory_space=SMEM)
    vmem = pl.BlockSpec(memory_space=VMEM)
    hbm = pl.BlockSpec(memory_space=pl.ANY)
    params = pltpu.CompilerParams(vmem_limit_bytes=56 << 20)

    def pack(*args):
        return pack_kernel(n_dev, *args)

    halo_shape = jax.ShapeDtypeStruct((HALO, width_c, width_b), BF16)
    packed = pl.pallas_call(
        pack, out_shape=(halo_shape,) * 4, in_specs=[smem, vmem], out_specs=(vmem,) * 4,
        scratch_shapes=[pltpu.VMEM((HALO + 1, width_c, width_b), BF16)] * 4, compiler_params=params, name="pack",
    )(nbr.T, prolong_t)
    up = lambda size: [(i, i + 1) for i in range(size - 1)]
    down = lambda size: [(i + 1, i) for i in range(size - 1)]
    from_low = lax.ppermute(packed[1], "grp", up(n_grp))
    from_high = lax.ppermute(packed[0], "grp", down(n_grp))
    from_left = lax.ppermute(packed[3], "dev", up(n_dev))
    from_right = lax.ppermute(packed[2], "dev", down(n_dev))

    def main(*args):
        return main_kernel(n_dev, rows_own, *args)

    outgoing = pl.pallas_call(
        main, out_shape=jax.ShapeDtypeStruct((n_dev, 8, width), BF16),
        in_specs=[smem] * 5 + [hbm, vmem] + [hbm] * 4, out_specs=vmem,
        scratch_shapes=[
            pltpu.VMEM((e_dev, BLOCKS, width_b, width_b), BF16),
            pltpu.VMEM((e_dev + 4 * HALO, width_c, width_b), BF16),
            pltpu.VMEM((TOUCH * 8 * width_c, LANES), F32),
            pltpu.VMEM((BLOCKS, width_c, width_b), BF16),
            pltpu.VMEM((BLOCKS, width_c, width_b), BF16),
            pltpu.SMEM((5 * e_dev,), jnp.int32),
            pltpu.SMEM((5 * e_dev,), jnp.int32),
            pltpu.SemaphoreType.DMA((e_dev,)),
            pltpu.SemaphoreType.DMA((4,)),
        ],
        compiler_params=params, name="products",
    )(elem_slot, nbr.T, nbr_agg.T, coarse_row, touch_agg.T, a_blocks, prolong_t, from_low, from_high, from_left, from_right)
    incoming = lax.all_to_all(outgoing, "dev", split_axis=0, concat_axis=0, tiled=True)
    piece = 8 * ((BLOCKS * group_rows) // 8 + 1)

    def combine(*args):
        return combine_kernel(rows_own, group_rows, *args)

    mine = pl.pallas_call(
        combine, out_shape=jax.ShapeDtypeStruct((piece, width), BF16), in_specs=[vmem], out_specs=vmem,
        scratch_shapes=[pltpu.SMEM((rows_own + 1,), jnp.int32), pltpu.SMEM((group_rows + 1,), jnp.int32)],
        compiler_params=params, name="combine",
    )(incoming.reshape(n_dev * 8, width))
    swap = [(i, i ^ 1) for i in range(n_grp)]
    across = [lax.ppermute(mine, "grp", [(i, (i + 2 * k) % n_grp) for i in range(n_grp)]) for k in range(1, n_grp // 2)]
    twin = lax.ppermute(mine, "grp", swap)
    others = lax.ppermute(jnp.stack(across), "grp", swap)
    pieces = (mine, twin, *across, others)

    def scatter(*args):
        return scatter_kernel(rows_own, group_rows, *args)

    out = pl.pallas_call(
        scatter, out_shape=jax.ShapeDtypeStruct((BLOCKS * rows_own, width), F32), in_specs=[hbm] * len(pieces),
        out_specs=hbm,
        scratch_shapes=[
            pltpu.VMEM((n_grp * piece, width), BF16),
            pltpu.VMEM((BLOCKS * rows_own, n_grp * piece), BF16),
            pltpu.VMEM((BLOCKS * rows_own, width), F32),
            pltpu.SemaphoreType.DMA((n_grp,)),
            pltpu.SemaphoreType.DMA((4,)),
        ],
        compiler_params=params, name="scatter",
    )(*pieces)
    return jnp.swapaxes(out.reshape(BLOCKS, rows_own, width), 0, 1)


def solution(mesh):
    in_specs = (
        P(("grp", "dev"), None, None, None),
        P(("grp", "dev"), None, None),
        P(("grp", "dev")),
        P(),
        P(("grp", "dev"), None),
        P(("grp", "dev"), None),
        P(),
    )
    return jax.shard_map(
        on_device, mesh=mesh, in_specs=in_specs, out_specs=P("dev", None, None), check_vma=False
    )
```

```python
import jax
import jax.numpy as jnp
from jax import lax
from jax.experimental import pallas as pl
from jax.experimental.pallas import tpu as pltpu
from jax.sharding import PartitionSpec as P

TOUCH = 6
FACES = 6
BLOCKS = 7
LANES = 128
HALO = 8
WINDOW = 8
SAME = 256
APART = 512
F32 = jnp.float32
BF16 = jnp.bfloat16
SMEM = pltpu.MemorySpace.SMEM
VMEM = pltpu.MemorySpace.VMEM


def position(n_dev):
    return lax.axis_index("grp") * n_dev + lax.axis_index("dev")


def pack_kernel(n_dev, nbr_ref, p_ref, *outs):
    e_dev = p_ref.shape[0]
    shift = e_dev.bit_length() - 1
    device = position(n_dev)
    homes = (device - n_dev, device + n_dev, device - 1, device + 1)

    def step(e, counts):
        hits = [jnp.bool_(False)] * 4
        for f in range(FACES):
            home = lax.shift_right_arithmetic(nbr_ref[f, e], shift)
            hits = [hit | (home == h) for hit, h in zip(hits, homes)]
        block = p_ref[e]
        new = []
        for d in range(4):
            outs[d][jnp.minimum(counts[d], HALO)] = block
            new.append(counts[d] + hits[d].astype(jnp.int32))
        return tuple(new)

    lax.fori_loop(0, e_dev, step, (jnp.int32(0),) * 4, unroll=4)


def route_kernel(n_dev, rows_own, slot_ref, nbr_ref, nagg_ref, touch_ref, crow_ref, out_ref):
    e_dev = slot_ref.shape[1]
    shift = e_dev.bit_length() - 1
    device = position(n_dev)
    nbr = nbr_ref[...]
    home = lax.shift_right_arithmetic(nbr, shift)
    local = nbr & (e_dev - 1)
    side = jnp.full(nbr.shape, 4, jnp.int32)
    for d, h in enumerate((device - n_dev, device + n_dev, device - 1, device + 1)):
        side = jnp.where(home == h, d, side)
    slot = slot_ref[...]
    own = jnp.zeros_like(slot)
    for t in range(TOUCH):
        own = jnp.where(slot == t, touch_ref[t, device], own)
    mode = jnp.where(nbr < 0, 0, jnp.where(nagg_ref[...] == own, SAME, APART))
    row = lax.broadcasted_iota(jnp.int32, (e_dev, e_dev), 0)
    seen = []
    for d in range(4):
        hit = jnp.zeros((e_dev, e_dev), F32)
        for f in range(FACES):
            hit = jnp.where((side[f : f + 1] == d) & (local[f : f + 1] == row), 1.0, hit)
        seen.append(jnp.max(hit, axis=1, keepdims=True))
    for f in range(FACES):
        there = jnp.zeros((e_dev, e_dev), F32)
        for d in range(4):
            there = jnp.where(side[f : f + 1] == d, seen[d], there)
        before = jnp.sum(jnp.where(row < local[f : f + 1], there, 0.0), axis=0, keepdims=True).astype(jnp.int32)
        halo = e_dev + HALO * side[f : f + 1] + jnp.minimum(before, HALO - 1)
        out_ref[f : f + 1, 0:e_dev] = jnp.where(side[f : f + 1] < 4, halo, local[f : f + 1]) + mode[f : f + 1]
    out_ref[FACES : FACES + 1, 0:e_dev] = slot
    lane = lax.broadcasted_iota(jnp.int32, (1, LANES), 1)
    rows = jnp.zeros((1, LANES), jnp.int32)
    for t in range(TOUCH):
        row = crow_ref[touch_ref[t, device]]
        owner = row // rows_own
        rows = jnp.where(lane == t, owner, jnp.where(lane == 8 + t, row - owner * rows_own + 1, rows))
    out_ref[FACES + 1 : FACES + 2] = rows


def main_kernel(route_ref, a_hbm, p_hbm, h0, h1, h2, h3,
                out_ref, abuf, pool, acc, lefts0, lefts1, a_sems, h_sems):
    e_dev, width_c, _ = p_hbm.shape

    def fetch(e):
        return pltpu.make_async_copy(a_hbm.at[e], abuf.at[e], a_sems.at[e])

    own_copy = pltpu.make_async_copy(p_hbm, pool.at[pl.ds(0, e_dev)], h_sems.at[4])
    own_copy.start()
    halos = [
        pltpu.make_async_copy(h.at[pl.ds(0, HALO)], pool.at[pl.ds(e_dev + HALO * d, HALO)], h_sems.at[d])
        for d, h in enumerate((h0, h1, h2, h3))
    ]
    for copy in halos:
        copy.start()
    for e in range(WINDOW):
        fetch(e).start()
    acc[...] = jnp.zeros_like(acc)
    out_ref[...] = jnp.zeros_like(out_ref)
    own_copy.wait()
    for copy in halos:
        copy.wait()

    def make_lefts(e, lefts):
        left = pool[e]
        for k in range(BLOCKS):
            lefts[k] = jnp.dot(left, abuf[e, k], preferred_element_type=F32).astype(BF16)

    def add_products(e, lefts):
        slot = route_ref[FACES, e]
        total = None
        for k in range(BLOCKS):
            if k == 0:
                right = pool[e]
            else:
                route = route_ref[k - 1, e]
                right = pool[route & (SAME - 1)]
            prod = lax.dot_general(lefts[k], right, (((1,), (1,)), ((), ())), preferred_element_type=F32)
            if k == 0:
                total = prod
                continue
            total = total + jnp.where((route & SAME) != 0, prod, 0.0)
            at = pl.multiple_of((slot * 8 + k) * width_c, width_c)
            acc[pl.ds(at, width_c), 0:width_c] += jnp.where((route & APART) != 0, prod, 0.0)
        at = pl.multiple_of(slot * 8 * width_c, width_c)
        acc[pl.ds(at, width_c), 0:width_c] += total

    fetch(0).wait()
    make_lefts(0, lefts0)

    def two(i, c):
        e = 2 * i + 1
        for ahead in range(2):

            @pl.when(e + ahead + WINDOW - 1 < e_dev)
            def _():
                fetch(e + ahead + WINDOW - 1).start()

        fetch(e).wait()
        fetch(e + 1).wait()
        add_products(e - 1, lefts0)
        make_lefts(e, lefts1)
        add_products(e, lefts1)
        make_lefts(e + 1, lefts0)
        return c

    lax.fori_loop(0, e_dev // 2 - 1, two, 0)
    fetch(e_dev - 1).wait()
    make_lefts(e_dev - 1, lefts1)
    add_products(e_dev - 2, lefts0)
    add_products(e_dev - 1, lefts1)

    lane = lax.broadcasted_iota(jnp.int32, (8, LANES), 1)
    sub = lax.broadcasted_iota(jnp.int32, (8, LANES), 0)
    per = LANES // width_c
    for t in range(TOUCH):
        owner = route_ref[FACES + 1, t]
        code = route_ref[FACES + 1, 8 + t].astype(F32)
        for j in range(width_c // per):
            value = None
            for i in range(per):
                piece = acc[pl.ds(t * 8 * width_c + j * per + i, 8, stride=width_c), :]
                if i == 0:
                    value = piece
                else:
                    piece = pltpu.roll(piece, i * width_c, 1)
                    value = jnp.where(lane >= i * width_c, piece, value)
            value = jnp.where(sub == 7, code, value)
            out_ref[owner, :, j * LANES : (j + 1) * LANES] = value.astype(BF16)


def combine_kernel(rows_own, group_rows, in_ref, out_ref, rank, codes):
    slots, width = in_ref.shape
    n_dev = slots // 8
    piece = out_ref.shape[0]

    def clear(i, c):
        rank[i] = -1
        return c

    lax.fori_loop(0, rows_own + 1, clear, 0, unroll=8)
    for r in range(group_rows + 1):
        codes[r] = 0
    used = jnp.int32(0)
    lane = lax.broadcasted_iota(jnp.int32, (1, slots), 1)
    key = jnp.full((1, slots), -1, jnp.int32)
    for d in range(n_dev):
        code = in_ref[8 * d : 8 * d + 8, 0:LANES].astype(F32)[7, 0].astype(jnp.int32)
        old = rank[code]
        fresh = (code > 0) & (old < 0)
        at = jnp.where(code > 0, jnp.where(old < 0, jnp.minimum(used, group_rows - 1), old), group_rows)
        rank[code] = jnp.where(code > 0, at, -1)
        codes[at] = code
        used = used + fresh.astype(jnp.int32)
        mine = (lane >= 8 * d) & (lane < 8 * d + 7)
        key = jnp.where(mine, jnp.where(code > 0, (lane - 8 * d) * group_rows + at, -1), key)
    row = lax.broadcasted_iota(jnp.int32, (piece, slots), 0)
    chosen = jnp.where(row == key, 1.0, 0.0).astype(BF16)
    out = jnp.dot(chosen, in_ref[...], preferred_element_type=F32)
    at = lax.broadcasted_iota(jnp.int32, (1, width), 1) % piece
    of_row = at % group_rows
    tags = jnp.zeros((1, width), F32)
    for r in range(group_rows):
        tags = jnp.where((of_row == r) & (at < BLOCKS * group_rows), codes[r].astype(F32), tags)
    rows = lax.broadcasted_iota(jnp.int32, (piece, width), 0)
    out_ref[...] = jnp.where(rows >= BLOCKS * group_rows, tags, out).astype(BF16)


def scatter_kernel(rows_own, group_rows, *refs):
    ins, out_hbm, held, chosen, out_buf, in_sems, out_sems = refs[:-6], *refs[-6:]
    total, width = out_buf.shape
    piece = ins[0].shape[-2]
    sources = [ref if len(ref.shape) == 2 else ref.at[q] for ref in ins for q in range(1 if len(ref.shape) == 2 else ref.shape[0])]
    copies = [
        pltpu.make_async_copy(ref, held.at[pl.ds(q * piece, piece)], in_sems.at[q]) for q, ref in enumerate(sources)
    ]
    for copy in copies:
        copy.start()
    depth = held.shape[0]
    lane = lax.broadcasted_iota(jnp.int32, (1, depth), 1)
    in_piece = lane % piece
    block = in_piece // group_rows
    for copy in copies:
        copy.wait()
    tags = jnp.zeros((1, depth), F32)
    for q in range(len(sources)):
        tag = held[(q + 1) * piece - 8 : (q + 1) * piece, 0:depth].astype(F32)[7:8]
        tags = jnp.where((lane >= q * piece) & (lane < (q + 1) * piece), tag, tags)
    tags = tags.astype(jnp.int32)
    key = jnp.where((tags > 0) & (block < BLOCKS), block * rows_own + tags - 1, -1)
    for s in range(BLOCKS):
        row = lax.broadcasted_iota(jnp.int32, (rows_own, depth), 0) + s * rows_own
        chosen[s * rows_own : (s + 1) * rows_own] = jnp.where(row == key, 1.0, 0.0).astype(BF16)
    n_out = out_sems.shape[0]
    step = width // n_out
    outs = []
    for n in range(n_out):
        cols = pl.ds(n * step, step)
        out_buf[:, n * step : (n + 1) * step] = jnp.dot(
            chosen[...], held[:, n * step : (n + 1) * step], preferred_element_type=F32
        )
        copy = pltpu.make_async_copy(out_buf.at[:, cols], out_hbm.at[:, cols], out_sems.at[n])
        copy.start()
        outs.append(copy)
    for copy in outs:
        copy.wait()


def on_device(a_blocks, prolong_t, elem_slot, touch_agg, nbr, nbr_agg, coarse_row):
    n_grp = lax.axis_size("grp")
    n_dev = lax.axis_size("dev")
    e_dev, width_c, width_b = prolong_t.shape
    half = 2
    group_rows = ((n_dev * half + 1) + half) // (half + 1)
    rows_own = n_grp * group_rows
    width = width_c * width_c
    smem = pl.BlockSpec(memory_space=SMEM)
    vmem = pl.BlockSpec(memory_space=VMEM)
    hbm = pl.BlockSpec(memory_space=pl.ANY)

    def params(mib):
        return pltpu.CompilerParams(vmem_limit_bytes=mib << 20)

    def pack(*args):
        return pack_kernel(n_dev, *args)

    halo_shape = jax.ShapeDtypeStruct((HALO + 1, width_c, width_b), BF16)
    packed = pl.pallas_call(
        pack, out_shape=(halo_shape,) * 4, in_specs=[smem, vmem], out_specs=(vmem,) * 4,
        compiler_params=params(56), name="pack",
    )(nbr.T, prolong_t)
    up = lambda size: [(i, (i + 1) % size) for i in range(size)]
    down = lambda size: [((i + 1) % size, i) for i in range(size)]
    from_low = lax.ppermute(packed[1], "grp", up(n_grp))
    from_high = lax.ppermute(packed[0], "grp", down(n_grp))
    from_left = lax.ppermute(packed[3], "dev", up(n_dev))
    from_right = lax.ppermute(packed[2], "dev", down(n_dev))

    def route(*args):
        return route_kernel(n_dev, rows_own, *args)

    routes = pl.pallas_call(
        route, out_shape=jax.ShapeDtypeStruct((8, LANES), jnp.int32), in_specs=[vmem] * 3 + [smem] * 2, out_specs=vmem,
        name="routes",
    )(elem_slot.reshape(1, e_dev), nbr.T, nbr_agg.T, touch_agg.T, coarse_row)

    outgoing = pl.pallas_call(
        main_kernel, out_shape=jax.ShapeDtypeStruct((n_dev, 8, width), BF16),
        in_specs=[smem] + [hbm] * 6, out_specs=vmem,
        scratch_shapes=[
            pltpu.VMEM((e_dev, BLOCKS, width_b, width_b), BF16),
            pltpu.VMEM((e_dev + 4 * HALO, width_c, width_b), BF16),
            pltpu.VMEM((TOUCH * 8 * width_c, LANES), F32),
            pltpu.VMEM((BLOCKS, width_c, width_b), BF16),
            pltpu.VMEM((BLOCKS, width_c, width_b), BF16),
            pltpu.SemaphoreType.DMA((e_dev,)),
            pltpu.SemaphoreType.DMA((5,)),
        ],
        compiler_params=params(56), name="products",
    )(routes, a_blocks, prolong_t, from_low, from_high, from_left, from_right)
    incoming = lax.all_to_all(outgoing, "dev", split_axis=0, concat_axis=0, tiled=True)
    piece = 8 * ((BLOCKS * group_rows) // 8 + 1)

    def combine(*args):
        return combine_kernel(rows_own, group_rows, *args)

    mine = pl.pallas_call(
        combine, out_shape=jax.ShapeDtypeStruct((piece, width), BF16), in_specs=[vmem], out_specs=vmem,
        scratch_shapes=[pltpu.SMEM((rows_own + 1,), jnp.int32), pltpu.SMEM((group_rows + 1,), jnp.int32)],
        compiler_params=params(8), name="combine",
    )(incoming.reshape(n_dev * 8, width))
    swap = [(i, i ^ 1) for i in range(n_grp)]
    across = [lax.ppermute(mine, "grp", [(i, (i + 2 * k) % n_grp) for i in range(n_grp)]) for k in range(1, n_grp // 2)]
    twin = lax.ppermute(mine, "grp", swap)
    others = [lax.ppermute(part, "grp", swap) for part in across]
    pieces = (mine, twin, *across, *others)

    def scatter(*args):
        return scatter_kernel(rows_own, group_rows, *args)

    out = pl.pallas_call(
        scatter, out_shape=jax.ShapeDtypeStruct((BLOCKS * rows_own, width), F32), in_specs=[hbm] * len(pieces),
        out_specs=hbm,
        scratch_shapes=[
            pltpu.VMEM((n_grp * piece, width), BF16),
            pltpu.VMEM((BLOCKS * rows_own, n_grp * piece), BF16),
            pltpu.VMEM((BLOCKS * rows_own, width), F32),
            pltpu.SemaphoreType.DMA((n_grp,)),
            pltpu.SemaphoreType.DMA((4,)),
        ],
        compiler_params=params(16), name="scatter",
    )(*pieces)
    return jnp.swapaxes(out.reshape(BLOCKS, rows_own, width), 0, 1)


def solution(mesh):
    in_specs = (
        P(("grp", "dev"), None, None, None),
        P(("grp", "dev"), None, None),
        P(("grp", "dev")),
        P(),
        P(("grp", "dev"), None),
        P(("grp", "dev"), None),
        P(),
    )
    return jax.shard_map(
        on_device, mesh=mesh, in_specs=in_specs, out_specs=P("dev", None, None), check_vma=False
    )
```

```python
import jax
import jax.numpy as jnp
from jax import lax
from jax.experimental import pallas as pl
from jax.experimental.pallas import tpu as pltpu
from jax.sharding import PartitionSpec as P

TOUCH = 6
FACES = 6
BLOCKS = 7
LANES = 128
HALO = 8
WINDOW = 8
EARLY = 8
SAME = 256
APART = 512
F32 = jnp.float32
BF16 = jnp.bfloat16
SMEM = pltpu.MemorySpace.SMEM
VMEM = pltpu.MemorySpace.VMEM


def position(n_dev):
    return lax.axis_index("grp") * n_dev + lax.axis_index("dev")


def load(pairs):
    copies = [pltpu.make_async_copy(src, dst, sem) for src, dst, sem in pairs]
    for copy in copies:
        copy.start()
    return copies


def pack_kernel(n_dev, nbr_hbm, p_hbm, *refs):
    outs, nbr_ref, p_ref, sems = refs[:4], *refs[4:]
    e_dev = p_ref.shape[0]
    quarter = e_dev // 4
    copies = load(
        [(nbr_hbm, nbr_ref, sems.at[4])]
        + [(p_hbm.at[pl.ds(i * quarter, quarter)], p_ref.at[pl.ds(i * quarter, quarter)], sems.at[i]) for i in range(4)]
    )
    for copy in copies:
        copy.wait()
    shift = e_dev.bit_length() - 1
    device = position(n_dev)
    homes = (device - n_dev, device + n_dev, device - 1, device + 1)

    def step(e, counts):
        hits = [jnp.bool_(False)] * 4
        for f in range(FACES):
            home = lax.shift_right_arithmetic(nbr_ref[f, e], shift)
            hits = [hit | (home == h) for hit, h in zip(hits, homes)]
        block = p_ref[e]
        new = []
        for d in range(4):
            outs[d][jnp.minimum(counts[d], HALO)] = block
            new.append(counts[d] + hits[d].astype(jnp.int32))
        return tuple(new)

    lax.fori_loop(0, e_dev, step, (jnp.int32(0),) * 4, unroll=4)


def early_kernel(n_dev, rows_own, slot_hbm, nbr_hbm, nagg_hbm, touch_hbm, crow_hbm, a_hbm, p_hbm, out_ref, lefts,
                 abuf, pbuf, slot_ref, nbr_ref, nagg_ref, touch_ref, crow_ref, a_sems, p_sem, sems):
    early = lefts.shape[0]
    small = load(
        [
            (slot_hbm, slot_ref, sems.at[0]),
            (nbr_hbm, nbr_ref, sems.at[1]),
            (nagg_hbm, nagg_ref, sems.at[2]),
            (touch_hbm, touch_ref, sems.at[3]),
            (crow_hbm, crow_ref, sems.at[4]),
        ]
    )

    def fetch(e):
        return pltpu.make_async_copy(a_hbm.at[e], abuf.at[e], a_sems.at[e])

    p_copy = pltpu.make_async_copy(p_hbm.at[pl.ds(0, early)], pbuf, p_sem)
    for e in range(early):
        fetch(e).start()
    p_copy.start()
    e_dev = slot_ref.shape[1]
    shift = e_dev.bit_length() - 1
    device = position(n_dev)
    for copy in small:
        copy.wait()
    nbr = nbr_ref[...]
    home = lax.shift_right_arithmetic(nbr, shift)
    local = nbr & (e_dev - 1)
    side = jnp.full(nbr.shape, 4, jnp.int32)
    for d, h in enumerate((device - n_dev, device + n_dev, device - 1, device + 1)):
        side = jnp.where(home == h, d, side)
    slot = slot_ref[...]
    own = jnp.zeros_like(slot)
    for t in range(TOUCH):
        own = jnp.where(slot == t, touch_ref[t, device], own)
    mode = jnp.where(nbr < 0, 0, jnp.where(nagg_ref[...] == own, SAME, APART))
    row = lax.broadcasted_iota(jnp.int32, (e_dev, e_dev), 0)
    seen = []
    for d in range(4):
        hit = jnp.zeros((e_dev, e_dev), F32)
        for f in range(FACES):
            hit = jnp.where((side[f : f + 1] == d) & (local[f : f + 1] == row), 1.0, hit)
        seen.append(jnp.max(hit, axis=1, keepdims=True))
    for f in range(FACES):
        there = jnp.zeros((e_dev, e_dev), F32)
        for d in range(4):
            there = jnp.where(side[f : f + 1] == d, seen[d], there)
        before = jnp.sum(jnp.where(row < local[f : f + 1], there, 0.0), axis=0, keepdims=True).astype(jnp.int32)
        halo = e_dev + HALO * side[f : f + 1] + jnp.minimum(before, HALO - 1)
        out_ref[f : f + 1, 0:e_dev] = jnp.where(side[f : f + 1] < 4, halo, local[f : f + 1]) + mode[f : f + 1]
    out_ref[FACES : FACES + 1, 0:e_dev] = slot
    lane = lax.broadcasted_iota(jnp.int32, (1, LANES), 1)
    rows = jnp.zeros((1, LANES), jnp.int32)
    for t in range(TOUCH):
        row = crow_ref[touch_ref[t, device]]
        owner = row // rows_own
        rows = jnp.where(lane == t, owner, jnp.where(lane == 8 + t, row - owner * rows_own + 1, rows))
    out_ref[FACES + 1 : FACES + 2] = rows
    p_copy.wait()

    def two(i, c):
        for e in (2 * i, 2 * i + 1):
            fetch(e).wait()
        for e in (2 * i, 2 * i + 1):
            for k in range(BLOCKS):
                lefts[e, k] = jnp.dot(pbuf[e], abuf[e, k], preferred_element_type=F32).astype(BF16)
        return c

    lax.fori_loop(0, early // 2, two, 0)


def main_kernel(route_hbm, a_hbm, p_hbm, early_hbm, h0, h1, h2, h3,
                out_ref, abuf, pool, acc, done, lefts0, lefts1, route_ref, a_sems, h_sems):
    e_dev, width_c, _ = p_hbm.shape
    early = done.shape[0]

    def fetch(e):
        return pltpu.make_async_copy(a_hbm.at[e], abuf.at[e - early], a_sems.at[e - early])

    own_copy = pltpu.make_async_copy(p_hbm, pool.at[pl.ds(0, e_dev)], h_sems.at[4])
    own_copy.start()
    route_copy = pltpu.make_async_copy(route_hbm, route_ref, h_sems.at[5])
    route_copy.start()
    done_copy = pltpu.make_async_copy(early_hbm, done, h_sems.at[6])
    done_copy.start()
    halos = [
        pltpu.make_async_copy(h.at[pl.ds(0, HALO)], pool.at[pl.ds(e_dev + HALO * d, HALO)], h_sems.at[d])
        for d, h in enumerate((h0, h1, h2, h3))
    ]
    for copy in halos:
        copy.start()
    for e in range(early, early + WINDOW):
        fetch(e).start()
    acc[...] = jnp.zeros_like(acc)
    out_ref[...] = jnp.zeros_like(out_ref)
    own_copy.wait()
    route_copy.wait()
    done_copy.wait()
    for copy in halos:
        copy.wait()

    def make_lefts(e, lefts):
        left = pool[e]
        for k in range(BLOCKS):
            lefts[k] = jnp.dot(left, abuf[e - early, k], preferred_element_type=F32).astype(BF16)

    def add_products(e, lefts):
        slot = route_ref[FACES, e]
        total = None
        for k in range(BLOCKS):
            if k == 0:
                right = pool[e]
            else:
                route = route_ref[k - 1, e]
                right = pool[route & (SAME - 1)]
            prod = lax.dot_general(lefts[k], right, (((1,), (1,)), ((), ())), preferred_element_type=F32)
            if k == 0:
                total = prod
                continue
            total = total + jnp.where((route & SAME) != 0, prod, 0.0)
            at = pl.multiple_of((slot * 8 + k) * width_c, width_c)
            acc[pl.ds(at, width_c), 0:width_c] += jnp.where((route & APART) != 0, prod, 0.0)
        at = pl.multiple_of(slot * 8 * width_c, width_c)
        acc[pl.ds(at, width_c), 0:width_c] += total

    def ready(i, c):
        for e in (2 * i, 2 * i + 1):
            add_products(e, done.at[e])
        return c

    lax.fori_loop(0, early // 2, ready, 0)
    fetch(early).wait()
    make_lefts(early, lefts0)

    def two(i, c):
        e = early + 2 * i + 1
        for ahead in range(2):

            @pl.when(e + ahead + WINDOW - 1 < e_dev)
            def _():
                fetch(e + ahead + WINDOW - 1).start()

        fetch(e).wait()
        fetch(e + 1).wait()
        add_products(e - 1, lefts0)
        make_lefts(e, lefts1)
        add_products(e, lefts1)
        make_lefts(e + 1, lefts0)
        return c

    lax.fori_loop(0, (e_dev - early) // 2 - 1, two, 0)
    fetch(e_dev - 1).wait()
    make_lefts(e_dev - 1, lefts1)
    add_products(e_dev - 2, lefts0)
    add_products(e_dev - 1, lefts1)

    lane = lax.broadcasted_iota(jnp.int32, (8, LANES), 1)
    sub = lax.broadcasted_iota(jnp.int32, (8, LANES), 0)
    per = LANES // width_c
    for t in range(TOUCH):
        owner = route_ref[FACES + 1, t]
        code = route_ref[FACES + 1, 8 + t].astype(F32)
        for j in range(width_c // per):
            value = None
            for i in range(per):
                piece = acc[pl.ds(t * 8 * width_c + j * per + i, 8, stride=width_c), :]
                if i == 0:
                    value = piece
                else:
                    piece = pltpu.roll(piece, i * width_c, 1)
                    value = jnp.where(lane >= i * width_c, piece, value)
            value = jnp.where(sub == 7, code, value)
            out_ref[owner, :, j * LANES : (j + 1) * LANES] = value.astype(BF16)


def combine_kernel(rows_own, group_rows, in_ref, out_ref, rank, codes):
    slots, width = in_ref.shape
    n_dev = slots // 8
    piece = out_ref.shape[0]

    def clear(i, c):
        rank[i] = -1
        return c

    lax.fori_loop(0, rows_own + 1, clear, 0, unroll=8)
    for r in range(group_rows + 1):
        codes[r] = 0
    used = jnp.int32(0)
    lane = lax.broadcasted_iota(jnp.int32, (1, slots), 1)
    key = jnp.full((1, slots), -1, jnp.int32)
    for d in range(n_dev):
        code = in_ref[8 * d : 8 * d + 8, 0:LANES].astype(F32)[7, 0].astype(jnp.int32)
        old = rank[code]
        fresh = (code > 0) & (old < 0)
        at = jnp.where(code > 0, jnp.where(old < 0, jnp.minimum(used, group_rows - 1), old), group_rows)
        rank[code] = jnp.where(code > 0, at, -1)
        codes[at] = code
        used = used + fresh.astype(jnp.int32)
        mine = (lane >= 8 * d) & (lane < 8 * d + 7)
        key = jnp.where(mine, jnp.where(code > 0, (lane - 8 * d) * group_rows + at, -1), key)
    row = lax.broadcasted_iota(jnp.int32, (piece, slots), 0)
    chosen = jnp.where(row == key, 1.0, 0.0).astype(BF16)
    out = jnp.dot(chosen, in_ref[...], preferred_element_type=F32)
    at = lax.broadcasted_iota(jnp.int32, (1, width), 1) % piece
    of_row = at % group_rows
    tags = jnp.zeros((1, width), F32)
    for r in range(group_rows):
        tags = jnp.where((of_row == r) & (at < BLOCKS * group_rows), codes[r].astype(F32), tags)
    rows = lax.broadcasted_iota(jnp.int32, (piece, width), 0)
    out_ref[...] = jnp.where(rows >= BLOCKS * group_rows, tags, out).astype(BF16)


def scatter_kernel(rows_own, group_rows, *refs):
    ins, out_hbm, held, chosen, out_buf, out_sems = refs[:-5], *refs[-5:]
    width = out_buf.shape[1]
    piece = ins[0].shape[0]
    depth = held.shape[0]
    for q, ref in enumerate(ins):
        held[q * piece : (q + 1) * piece] = ref[...]
    lane = lax.broadcasted_iota(jnp.int32, (1, depth), 1)
    in_piece = lane % piece
    block = in_piece // group_rows
    tags = jnp.zeros((1, depth), F32)
    for q, ref in enumerate(ins):
        tag = ref[piece - 8 : piece, 0:depth].astype(F32)[7:8]
        tags = jnp.where((lane >= q * piece) & (lane < (q + 1) * piece), tag, tags)
    tags = tags.astype(jnp.int32)
    key = jnp.where((tags > 0) & (block < BLOCKS), block * rows_own + tags - 1, -1)
    for s in range(BLOCKS):
        row = lax.broadcasted_iota(jnp.int32, (rows_own, depth), 0) + s * rows_own
        chosen[s * rows_own : (s + 1) * rows_own] = jnp.where(row == key, 1.0, 0.0).astype(BF16)
    n_out = out_sems.shape[0]
    step = width // n_out
    outs = []
    for n in range(n_out):
        cols = pl.ds(n * step, step)
        out_buf[:, n * step : (n + 1) * step] = jnp.dot(
            chosen[...], held[:, n * step : (n + 1) * step], preferred_element_type=F32
        )
        copy = pltpu.make_async_copy(out_buf.at[:, cols], out_hbm.at[:, cols], out_sems.at[n])
        copy.start()
        outs.append(copy)
    for copy in outs:
        copy.wait()


def on_device(a_blocks, prolong_t, elem_slot, touch_agg, nbr, nbr_agg, coarse_row):
    n_grp = lax.axis_size("grp")
    n_dev = lax.axis_size("dev")
    e_dev, width_c, width_b = prolong_t.shape
    half = 2
    group_rows = ((n_dev * half + 1) + half) // (half + 1)
    rows_own = n_grp * group_rows
    width = width_c * width_c
    smem = pl.BlockSpec(memory_space=SMEM)
    vmem = pl.BlockSpec(memory_space=VMEM)
    hbm = pl.BlockSpec(memory_space=pl.ANY)

    def params(mib):
        return pltpu.CompilerParams(vmem_limit_bytes=mib << 20)

    def pack(*args):
        return pack_kernel(n_dev, *args)

    halo_shape = jax.ShapeDtypeStruct((HALO + 1, width_c, width_b), BF16)
    packed = pl.pallas_call(
        pack, out_shape=(halo_shape,) * 4, in_specs=[hbm] * 2, out_specs=(vmem,) * 4,
        scratch_shapes=[pltpu.SMEM((FACES, e_dev), jnp.int32), pltpu.VMEM((e_dev, width_c, width_b), BF16),
                        pltpu.SemaphoreType.DMA((5,))],
        compiler_params=params(56), name="pack",
    )(nbr.T, prolong_t)
    up = lambda size: [(i, (i + 1) % size) for i in range(size)]
    down = lambda size: [((i + 1) % size, i) for i in range(size)]
    from_low = lax.ppermute(packed[1], "grp", up(n_grp))
    from_high = lax.ppermute(packed[0], "grp", down(n_grp))
    from_left = lax.ppermute(packed[3], "dev", up(n_dev))
    from_right = lax.ppermute(packed[2], "dev", down(n_dev))

    def early(*args):
        return early_kernel(n_dev, rows_own, *args)

    routes, lefts = pl.pallas_call(
        early,
        out_shape=(jax.ShapeDtypeStruct((8, LANES), jnp.int32), jax.ShapeDtypeStruct((EARLY, BLOCKS, width_c, width_b), BF16)),
        in_specs=[hbm] * 7, out_specs=(vmem, vmem),
        scratch_shapes=[
            pltpu.VMEM((EARLY, BLOCKS, width_b, width_b), BF16),
            pltpu.VMEM((EARLY, width_c, width_b), BF16),
            pltpu.VMEM((1, e_dev), jnp.int32),
            pltpu.VMEM((FACES, e_dev), jnp.int32),
            pltpu.VMEM((FACES, e_dev), jnp.int32),
            pltpu.SMEM(touch_agg.T.shape, jnp.int32),
            pltpu.SMEM(coarse_row.shape, jnp.int32),
            pltpu.SemaphoreType.DMA((EARLY,)),
            pltpu.SemaphoreType.DMA(()),
            pltpu.SemaphoreType.DMA((5,)),
        ],
        compiler_params=params(56), name="early",
    )(elem_slot.reshape(1, e_dev), nbr.T, nbr_agg.T, touch_agg.T, coarse_row, a_blocks, prolong_t)

    outgoing = pl.pallas_call(
        main_kernel, out_shape=jax.ShapeDtypeStruct((n_dev, 8, width), BF16),
        in_specs=[hbm] * 8, out_specs=vmem,
        scratch_shapes=[
            pltpu.VMEM((e_dev - EARLY, BLOCKS, width_b, width_b), BF16),
            pltpu.VMEM((e_dev + 4 * HALO, width_c, width_b), BF16),
            pltpu.VMEM((TOUCH * 8 * width_c, LANES), F32),
            pltpu.VMEM((EARLY, BLOCKS, width_c, width_b), BF16),
            pltpu.VMEM((BLOCKS, width_c, width_b), BF16),
            pltpu.VMEM((BLOCKS, width_c, width_b), BF16),
            pltpu.SMEM((8, LANES), jnp.int32),
            pltpu.SemaphoreType.DMA((e_dev - EARLY,)),
            pltpu.SemaphoreType.DMA((7,)),
        ],
        compiler_params=params(56), name="products",
    )(routes, a_blocks, prolong_t, lefts, from_low, from_high, from_left, from_right)
    incoming = lax.all_to_all(outgoing, "dev", split_axis=0, concat_axis=0, tiled=True)
    piece = 8 * ((BLOCKS * group_rows) // 8 + 1)

    def combine(*args):
        return combine_kernel(rows_own, group_rows, *args)

    mine = pl.pallas_call(
        combine, out_shape=jax.ShapeDtypeStruct((piece, width), BF16), in_specs=[vmem], out_specs=vmem,
        scratch_shapes=[pltpu.SMEM((rows_own + 1,), jnp.int32), pltpu.SMEM((group_rows + 1,), jnp.int32)],
        compiler_params=params(8), name="combine",
    )(incoming.reshape(n_dev * 8, width))
    swap = [(i, i ^ 1) for i in range(n_grp)]
    across = [lax.ppermute(mine, "grp", [(i, (i + 2 * k) % n_grp) for i in range(n_grp)]) for k in range(1, n_grp // 2)]
    twin = lax.ppermute(mine, "grp", swap)
    others = [lax.ppermute(part, "grp", swap) for part in across]
    pieces = (mine, twin, *across, *others)

    def scatter(*args):
        return scatter_kernel(rows_own, group_rows, *args)

    out = pl.pallas_call(
        scatter, out_shape=jax.ShapeDtypeStruct((BLOCKS * rows_own, width), F32), in_specs=[vmem] * len(pieces),
        out_specs=hbm,
        scratch_shapes=[
            pltpu.VMEM((n_grp * piece, width), BF16),
            pltpu.VMEM((BLOCKS * rows_own, n_grp * piece), BF16),
            pltpu.VMEM((BLOCKS * rows_own, width), F32),
            pltpu.SemaphoreType.DMA((4,)),
        ],
        compiler_params=params(16), name="scatter",
    )(*pieces)
    return jnp.swapaxes(out.reshape(BLOCKS, rows_own, width), 0, 1)


def solution(mesh):
    in_specs = (
        P(("grp", "dev"), None, None, None),
        P(("grp", "dev"), None, None),
        P(("grp", "dev")),
        P(),
        P(("grp", "dev"), None),
        P(("grp", "dev"), None),
        P(),
    )
    return jax.shard_map(
        on_device, mesh=mesh, in_specs=in_specs, out_specs=P("dev", None, None), check_vma=False
    )
```

```python
import jax
import jax.numpy as jnp
from jax import lax
from jax.experimental import pallas as pl
from jax.experimental.pallas import tpu as pltpu
from jax.sharding import PartitionSpec as P

TOUCH = 6
FACES = 6
BLOCKS = 7
LANES = 128
HALO = 8
WINDOW = 8
EARLY = 12
SAME = 256
APART = 512
F32 = jnp.float32
BF16 = jnp.bfloat16
SMEM = pltpu.MemorySpace.SMEM
VMEM = pltpu.MemorySpace.VMEM


def position(n_dev):
    return lax.axis_index("grp") * n_dev + lax.axis_index("dev")


def load(pairs):
    copies = [pltpu.make_async_copy(src, dst, sem) for src, dst, sem in pairs]
    for copy in copies:
        copy.start()
    return copies


def pack_kernel(n_dev, nbr_hbm, p_hbm, *refs):
    outs, nbr_ref, p_ref, sems = refs[:4], *refs[4:]
    e_dev = p_ref.shape[0]
    quarter = e_dev // 4
    copies = load(
        [(nbr_hbm, nbr_ref, sems.at[4])]
        + [(p_hbm.at[pl.ds(i * quarter, quarter)], p_ref.at[pl.ds(i * quarter, quarter)], sems.at[i]) for i in range(4)]
    )
    for copy in copies:
        copy.wait()
    shift = e_dev.bit_length() - 1
    device = position(n_dev)
    homes = (device - n_dev, device + n_dev, device - 1, device + 1)

    def step(e, counts):
        hits = [jnp.bool_(False)] * 4
        for f in range(FACES):
            home = lax.shift_right_arithmetic(nbr_ref[f, e], shift)
            hits = [hit | (home == h) for hit, h in zip(hits, homes)]
        block = p_ref[e]
        new = []
        for d in range(4):
            outs[d][jnp.minimum(counts[d], HALO)] = block
            new.append(counts[d] + hits[d].astype(jnp.int32))
        return tuple(new)

    lax.fori_loop(0, e_dev, step, (jnp.int32(0),) * 4, unroll=4)


def early_kernel(n_dev, rows_own, slot_hbm, nbr_hbm, nagg_hbm, touch_hbm, crow_hbm, a_hbm, p_hbm, out_ref, lefts,
                 abuf, pbuf, slot_ref, nbr_ref, nagg_ref, touch_ref, crow_ref, a_sems, p_sem, sems):
    early = lefts.shape[0]
    small = load(
        [
            (slot_hbm, slot_ref, sems.at[0]),
            (nbr_hbm, nbr_ref, sems.at[1]),
            (nagg_hbm, nagg_ref, sems.at[2]),
            (touch_hbm, touch_ref, sems.at[3]),
            (crow_hbm, crow_ref, sems.at[4]),
        ]
    )

    def fetch(e):
        return pltpu.make_async_copy(a_hbm.at[e], abuf.at[e], a_sems.at[e])

    p_copy = pltpu.make_async_copy(p_hbm.at[pl.ds(0, early)], pbuf, p_sem)
    for e in range(early):
        fetch(e).start()
    p_copy.start()
    e_dev = slot_ref.shape[1]
    shift = e_dev.bit_length() - 1
    device = position(n_dev)
    for copy in small:
        copy.wait()
    nbr = nbr_ref[...]
    home = lax.shift_right_arithmetic(nbr, shift)
    local = nbr & (e_dev - 1)
    side = jnp.full(nbr.shape, 4, jnp.int32)
    for d, h in enumerate((device - n_dev, device + n_dev, device - 1, device + 1)):
        side = jnp.where(home == h, d, side)
    slot = slot_ref[...]
    own = jnp.zeros_like(slot)
    for t in range(TOUCH):
        own = jnp.where(slot == t, touch_ref[t, device], own)
    mode = jnp.where(nbr < 0, 0, jnp.where(nagg_ref[...] == own, SAME, APART))
    row = lax.broadcasted_iota(jnp.int32, (e_dev, e_dev), 0)
    seen = []
    for d in range(4):
        hit = jnp.zeros((e_dev, e_dev), F32)
        for f in range(FACES):
            hit = jnp.where((side[f : f + 1] == d) & (local[f : f + 1] == row), 1.0, hit)
        seen.append(jnp.max(hit, axis=1, keepdims=True))
    for f in range(FACES):
        there = jnp.zeros((e_dev, e_dev), F32)
        for d in range(4):
            there = jnp.where(side[f : f + 1] == d, seen[d], there)
        before = jnp.sum(jnp.where(row < local[f : f + 1], there, 0.0), axis=0, keepdims=True).astype(jnp.int32)
        halo = e_dev + HALO * side[f : f + 1] + jnp.minimum(before, HALO - 1)
        out_ref[f : f + 1, 0:e_dev] = jnp.where(side[f : f + 1] < 4, halo, local[f : f + 1]) + mode[f : f + 1]
    out_ref[FACES : FACES + 1, 0:e_dev] = slot
    lane = lax.broadcasted_iota(jnp.int32, (1, LANES), 1)
    rows = jnp.zeros((1, LANES), jnp.int32)
    for t in range(TOUCH):
        row = crow_ref[touch_ref[t, device]]
        owner = row // rows_own
        rows = jnp.where(lane == t, owner, jnp.where(lane == 8 + t, row - owner * rows_own + 1, rows))
    out_ref[FACES + 1 : FACES + 2] = rows
    p_copy.wait()

    def four(i, c):
        for j in range(4):
            fetch(4 * i + j).wait()
        for j in range(4):
            e = 4 * i + j
            for k in range(BLOCKS):
                lefts[e, k] = jnp.dot(pbuf[e], abuf[e, k], preferred_element_type=F32).astype(BF16)
        return c

    lax.fori_loop(0, early // 4, four, 0)


def main_kernel(route_hbm, a_hbm, p_hbm, done, h0, h1, h2, h3,
                out_ref, abuf, pool, acc, lefts0, lefts1, route_ref, a_sems, h_sems):
    e_dev, width_c, _ = p_hbm.shape
    early = done.shape[0]

    def fetch(e):
        return pltpu.make_async_copy(a_hbm.at[e], abuf.at[e - early], a_sems.at[e - early])

    own_copy = pltpu.make_async_copy(p_hbm, pool.at[pl.ds(0, e_dev)], h_sems.at[4])
    own_copy.start()
    route_copy = pltpu.make_async_copy(route_hbm, route_ref, h_sems.at[5])
    route_copy.start()
    halos = [
        pltpu.make_async_copy(h.at[pl.ds(0, HALO)], pool.at[pl.ds(e_dev + HALO * d, HALO)], h_sems.at[d])
        for d, h in enumerate((h0, h1, h2, h3))
    ]
    for copy in halos:
        copy.start()
    for e in range(early, early + WINDOW):
        fetch(e).start()
    acc[...] = jnp.zeros_like(acc)
    out_ref[...] = jnp.zeros_like(out_ref)
    own_copy.wait()
    route_copy.wait()
    for copy in halos:
        copy.wait()

    def make_lefts(e, lefts):
        left = pool[e]
        for k in range(BLOCKS):
            lefts[k] = jnp.dot(left, abuf[e - early, k], preferred_element_type=F32).astype(BF16)

    def add_products(e, lefts):
        slot = route_ref[FACES, e]
        total = None
        for k in range(BLOCKS):
            if k == 0:
                right = pool[e]
            else:
                route = route_ref[k - 1, e]
                right = pool[route & (SAME - 1)]
            prod = lax.dot_general(lefts[k], right, (((1,), (1,)), ((), ())), preferred_element_type=F32)
            if k == 0:
                total = prod
                continue
            total = total + jnp.where((route & SAME) != 0, prod, 0.0)
            at = pl.multiple_of((slot * 8 + k) * width_c, width_c)
            acc[pl.ds(at, width_c), 0:width_c] += jnp.where((route & APART) != 0, prod, 0.0)
        at = pl.multiple_of(slot * 8 * width_c, width_c)
        acc[pl.ds(at, width_c), 0:width_c] += total

    def ready(i, c):
        for j in range(4):
            add_products(4 * i + j, done.at[4 * i + j])
        return c

    lax.fori_loop(0, early // 4, ready, 0)
    fetch(early).wait()
    make_lefts(early, lefts0)

    def two(i, c):
        e = early + 2 * i + 1
        for ahead in range(2):

            @pl.when(e + ahead + WINDOW - 1 < e_dev)
            def _():
                fetch(e + ahead + WINDOW - 1).start()

        fetch(e).wait()
        fetch(e + 1).wait()
        add_products(e - 1, lefts0)
        make_lefts(e, lefts1)
        add_products(e, lefts1)
        make_lefts(e + 1, lefts0)
        return c

    lax.fori_loop(0, (e_dev - early) // 2 - 1, two, 0)
    fetch(e_dev - 1).wait()
    make_lefts(e_dev - 1, lefts1)
    add_products(e_dev - 2, lefts0)
    add_products(e_dev - 1, lefts1)

    lane = lax.broadcasted_iota(jnp.int32, (8, LANES), 1)
    sub = lax.broadcasted_iota(jnp.int32, (8, LANES), 0)
    per = LANES // width_c
    for t in range(TOUCH):
        owner = route_ref[FACES + 1, t]
        code = route_ref[FACES + 1, 8 + t].astype(F32)
        for j in range(width_c // per):
            value = None
            for i in range(per):
                piece = acc[pl.ds(t * 8 * width_c + j * per + i, 8, stride=width_c), :]
                if i == 0:
                    value = piece
                else:
                    piece = pltpu.roll(piece, i * width_c, 1)
                    value = jnp.where(lane >= i * width_c, piece, value)
            value = jnp.where(sub == 7, code, value)
            out_ref[owner, :, j * LANES : (j + 1) * LANES] = value.astype(BF16)


def combine_kernel(rows_own, group_rows, in_ref, out_ref, rank, codes):
    slots, width = in_ref.shape
    n_dev = slots // 8
    piece = out_ref.shape[0]

    def clear(i, c):
        rank[i] = -1
        return c

    lax.fori_loop(0, rows_own + 1, clear, 0, unroll=8)
    for r in range(group_rows + 1):
        codes[r] = 0
    used = jnp.int32(0)
    lane = lax.broadcasted_iota(jnp.int32, (1, slots), 1)
    key = jnp.full((1, slots), -1, jnp.int32)
    for d in range(n_dev):
        code = in_ref[8 * d : 8 * d + 8, 0:LANES].astype(F32)[7, 0].astype(jnp.int32)
        old = rank[code]
        fresh = (code > 0) & (old < 0)
        at = jnp.where(code > 0, jnp.where(old < 0, jnp.minimum(used, group_rows - 1), old), group_rows)
        rank[code] = jnp.where(code > 0, at, -1)
        codes[at] = code
        used = used + fresh.astype(jnp.int32)
        mine = (lane >= 8 * d) & (lane < 8 * d + 7)
        key = jnp.where(mine, jnp.where(code > 0, (lane - 8 * d) * group_rows + at, -1), key)
    row = lax.broadcasted_iota(jnp.int32, (piece, slots), 0)
    chosen = jnp.where(row == key, 1.0, 0.0).astype(BF16)
    out = jnp.dot(chosen, in_ref[...], preferred_element_type=F32)
    at = lax.broadcasted_iota(jnp.int32, (1, width), 1) % piece
    of_row = at % group_rows
    tags = jnp.zeros((1, width), F32)
    for r in range(group_rows):
        tags = jnp.where((of_row == r) & (at < BLOCKS * group_rows), codes[r].astype(F32), tags)
    rows = lax.broadcasted_iota(jnp.int32, (piece, width), 0)
    out_ref[...] = jnp.where(rows >= BLOCKS * group_rows, tags, out).astype(BF16)


def scatter_kernel(rows_own, group_rows, *refs):
    ins, out_hbm, held, chosen, out_buf, out_sems = refs[:-5], *refs[-5:]
    width = out_buf.shape[1]
    piece = ins[0].shape[0]
    depth = held.shape[0]
    for q, ref in enumerate(ins):
        held[q * piece : (q + 1) * piece] = ref[...]
    lane = lax.broadcasted_iota(jnp.int32, (1, depth), 1)
    in_piece = lane % piece
    block = in_piece // group_rows
    tags = jnp.zeros((1, depth), F32)
    for q, ref in enumerate(ins):
        tag = ref[piece - 8 : piece, 0:depth].astype(F32)[7:8]
        tags = jnp.where((lane >= q * piece) & (lane < (q + 1) * piece), tag, tags)
    tags = tags.astype(jnp.int32)
    key = jnp.where((tags > 0) & (block < BLOCKS), block * rows_own + tags - 1, -1)
    for s in range(BLOCKS):
        row = lax.broadcasted_iota(jnp.int32, (rows_own, depth), 0) + s * rows_own
        chosen[s * rows_own : (s + 1) * rows_own] = jnp.where(row == key, 1.0, 0.0).astype(BF16)
    n_out = out_sems.shape[0]
    step = width // n_out
    outs = []
    for n in range(n_out):
        cols = pl.ds(n * step, step)
        out_buf[:, n * step : (n + 1) * step] = jnp.dot(
            chosen[...], held[:, n * step : (n + 1) * step], preferred_element_type=F32
        )
        copy = pltpu.make_async_copy(out_buf.at[:, cols], out_hbm.at[:, cols], out_sems.at[n])
        copy.start()
        outs.append(copy)
    for copy in outs:
        copy.wait()


def on_device(a_blocks, prolong_t, elem_slot, touch_agg, nbr, nbr_agg, coarse_row):
    n_grp = lax.axis_size("grp")
    n_dev = lax.axis_size("dev")
    e_dev, width_c, width_b = prolong_t.shape
    half = 2
    group_rows = ((n_dev * half + 1) + half) // (half + 1)
    rows_own = n_grp * group_rows
    width = width_c * width_c
    pin = lambda x: pltpu.with_memory_space_constraint(x, pltpu.MemorySpace.HBM)
    smem = pl.BlockSpec(memory_space=SMEM)
    vmem = pl.BlockSpec(memory_space=VMEM)
    hbm = pl.BlockSpec(memory_space=pl.ANY)

    def params(mib):
        return pltpu.CompilerParams(vmem_limit_bytes=mib << 20)

    def pack(*args):
        return pack_kernel(n_dev, *args)

    halo_shape = jax.ShapeDtypeStruct((HALO + 1, width_c, width_b), BF16)
    packed = pl.pallas_call(
        pack, out_shape=(halo_shape,) * 4, in_specs=[hbm] * 2, out_specs=(vmem,) * 4,
        scratch_shapes=[pltpu.SMEM((FACES, e_dev), jnp.int32), pltpu.VMEM((e_dev, width_c, width_b), BF16),
                        pltpu.SemaphoreType.DMA((5,))],
        compiler_params=params(8), name="pack",
    )(pin(nbr.T), pin(prolong_t))
    up = lambda size: [(i, (i + 1) % size) for i in range(size)]
    down = lambda size: [((i + 1) % size, i) for i in range(size)]
    from_low = lax.ppermute(packed[1], "grp", up(n_grp))
    from_high = lax.ppermute(packed[0], "grp", down(n_grp))
    from_left = lax.ppermute(packed[3], "dev", up(n_dev))
    from_right = lax.ppermute(packed[2], "dev", down(n_dev))

    def early(*args):
        return early_kernel(n_dev, rows_own, *args)

    routes, lefts = pl.pallas_call(
        early,
        out_shape=(jax.ShapeDtypeStruct((8, LANES), jnp.int32), jax.ShapeDtypeStruct((EARLY, BLOCKS, width_c, width_b), BF16)),
        in_specs=[hbm] * 7, out_specs=(vmem, vmem),
        scratch_shapes=[
            pltpu.VMEM((EARLY, BLOCKS, width_b, width_b), BF16),
            pltpu.VMEM((EARLY, width_c, width_b), BF16),
            pltpu.VMEM((1, e_dev), jnp.int32),
            pltpu.VMEM((FACES, e_dev), jnp.int32),
            pltpu.VMEM((FACES, e_dev), jnp.int32),
            pltpu.SMEM(touch_agg.T.shape, jnp.int32),
            pltpu.SMEM(coarse_row.shape, jnp.int32),
            pltpu.SemaphoreType.DMA((EARLY,)),
            pltpu.SemaphoreType.DMA(()),
            pltpu.SemaphoreType.DMA((5,)),
        ],
        compiler_params=params(14), name="early",
    )(*map(pin, (elem_slot.reshape(1, e_dev), nbr.T, nbr_agg.T, touch_agg.T, coarse_row, a_blocks, prolong_t)))

    outgoing = pl.pallas_call(
        main_kernel, out_shape=jax.ShapeDtypeStruct((n_dev, 8, width), BF16),
        in_specs=[hbm] * 3 + [vmem] + [hbm] * 4, out_specs=vmem,
        scratch_shapes=[
            pltpu.VMEM((e_dev - EARLY, BLOCKS, width_b, width_b), BF16),
            pltpu.VMEM((e_dev + 4 * HALO, width_c, width_b), BF16),
            pltpu.VMEM((TOUCH * 8 * width_c, LANES), F32),
            pltpu.VMEM((BLOCKS, width_c, width_b), BF16),
            pltpu.VMEM((BLOCKS, width_c, width_b), BF16),
            pltpu.SMEM((8, LANES), jnp.int32),
            pltpu.SemaphoreType.DMA((e_dev - EARLY,)),
            pltpu.SemaphoreType.DMA((6,)),
        ],
        compiler_params=params(36), name="products",
    )(routes, pin(a_blocks), pin(prolong_t), lefts, from_low, from_high, from_left, from_right)
    incoming = lax.all_to_all(outgoing, "dev", split_axis=0, concat_axis=0, tiled=True)
    piece = 8 * ((BLOCKS * group_rows) // 8 + 1)

    def combine(*args):
        return combine_kernel(rows_own, group_rows, *args)

    mine = pl.pallas_call(
        combine, out_shape=jax.ShapeDtypeStruct((piece, width), BF16), in_specs=[vmem], out_specs=vmem,
        scratch_shapes=[pltpu.SMEM((rows_own + 1,), jnp.int32), pltpu.SMEM((group_rows + 1,), jnp.int32)],
        compiler_params=params(8), name="combine",
    )(incoming.reshape(n_dev * 8, width))
    swap = [(i, i ^ 1) for i in range(n_grp)]
    across = [lax.ppermute(mine, "grp", [(i, (i + 2 * k) % n_grp) for i in range(n_grp)]) for k in range(1, n_grp // 2)]
    twin = lax.ppermute(mine, "grp", swap)
    others = [lax.ppermute(part, "grp", swap) for part in across]
    pieces = (mine, twin, *across, *others)

    def scatter(*args):
        return scatter_kernel(rows_own, group_rows, *args)

    out = pl.pallas_call(
        scatter, out_shape=jax.ShapeDtypeStruct((BLOCKS * rows_own, width), F32), in_specs=[vmem] * len(pieces),
        out_specs=hbm,
        scratch_shapes=[
            pltpu.VMEM((n_grp * piece, width), BF16),
            pltpu.VMEM((BLOCKS * rows_own, n_grp * piece), BF16),
            pltpu.VMEM((BLOCKS * rows_own, width), F32),
            pltpu.SemaphoreType.DMA((4,)),
        ],
        compiler_params=params(16), name="scatter",
    )(*pieces)
    return jnp.swapaxes(out.reshape(BLOCKS, rows_own, width), 0, 1)


def solution(mesh):
    in_specs = (
        P(("grp", "dev"), None, None, None),
        P(("grp", "dev"), None, None),
        P(("grp", "dev")),
        P(),
        P(("grp", "dev"), None),
        P(("grp", "dev"), None),
        P(),
    )
    return jax.shard_map(
        on_device, mesh=mesh, in_specs=in_specs, out_specs=P("dev", None, None), check_vma=False
    )
```

```python
import jax
import jax.numpy as jnp
from jax import lax
from jax.experimental import pallas as pl
from jax.experimental.pallas import tpu as pltpu
from jax.sharding import PartitionSpec as P

TOUCH = 6
FACES = 6
BLOCKS = 7
LANES = 128
HALO = 8
WINDOW = 8
EARLY = 16
SAME = 256
APART = 512
F32 = jnp.float32
BF16 = jnp.bfloat16
SMEM = pltpu.MemorySpace.SMEM
VMEM = pltpu.MemorySpace.VMEM


def position(n_dev):
    return lax.axis_index("grp") * n_dev + lax.axis_index("dev")


def load(pairs):
    copies = [pltpu.make_async_copy(src, dst, sem) for src, dst, sem in pairs]
    for copy in copies:
        copy.start()
    return copies


def pack_kernel(n_dev, nbr_hbm, p_hbm, *refs):
    outs, nbr_ref, p_ref, sems = refs[:4], *refs[4:]
    e_dev = p_ref.shape[0]
    quarter = e_dev // 4
    copies = load(
        [(nbr_hbm, nbr_ref, sems.at[4])]
        + [(p_hbm.at[pl.ds(i * quarter, quarter)], p_ref.at[pl.ds(i * quarter, quarter)], sems.at[i]) for i in range(4)]
    )
    for copy in copies:
        copy.wait()
    shift = e_dev.bit_length() - 1
    device = position(n_dev)
    homes = (device - n_dev, device + n_dev, device - 1, device + 1)

    def step(e, counts):
        hits = [jnp.bool_(False)] * 4
        for f in range(FACES):
            home = lax.shift_right_arithmetic(nbr_ref[f, e], shift)
            hits = [hit | (home == h) for hit, h in zip(hits, homes)]
        block = p_ref[e]
        new = []
        for d in range(4):
            outs[d][jnp.minimum(counts[d], HALO)] = block
            new.append(counts[d] + hits[d].astype(jnp.int32))
        return tuple(new)

    lax.fori_loop(0, e_dev, step, (jnp.int32(0),) * 4, unroll=16)


def early_kernel(n_dev, rows_own, slot_hbm, nbr_hbm, nagg_hbm, touch_hbm, crow_hbm, a_hbm, p_hbm, out_ref, lefts,
                 abuf, pbuf, slot_ref, nbr_ref, nagg_ref, touch_ref, crow_ref, a_sems, p_sem, sems):
    early = lefts.shape[0]
    small = load(
        [
            (slot_hbm, slot_ref, sems.at[0]),
            (nbr_hbm, nbr_ref, sems.at[1]),
            (nagg_hbm, nagg_ref, sems.at[2]),
            (touch_hbm, touch_ref, sems.at[3]),
            (crow_hbm, crow_ref, sems.at[4]),
        ]
    )

    def fetch(e):
        return pltpu.make_async_copy(a_hbm.at[e], abuf.at[e], a_sems.at[e])

    p_copy = pltpu.make_async_copy(p_hbm.at[pl.ds(0, early)], pbuf, p_sem)
    for e in range(early):
        fetch(e).start()
    p_copy.start()
    e_dev = slot_ref.shape[1]
    shift = e_dev.bit_length() - 1
    device = position(n_dev)
    for copy in small:
        copy.wait()
    nbr = nbr_ref[...]
    home = lax.shift_right_arithmetic(nbr, shift)
    local = nbr & (e_dev - 1)
    side = jnp.full(nbr.shape, 4, jnp.int32)
    for d, h in enumerate((device - n_dev, device + n_dev, device - 1, device + 1)):
        side = jnp.where(home == h, d, side)
    slot = slot_ref[...]
    own = jnp.zeros_like(slot)
    for t in range(TOUCH):
        own = jnp.where(slot == t, touch_ref[t, device], own)
    mode = jnp.where(nbr < 0, 0, jnp.where(nagg_ref[...] == own, SAME, APART))
    row = lax.broadcasted_iota(jnp.int32, (e_dev, e_dev), 0)
    seen = []
    for d in range(4):
        hit = jnp.zeros((e_dev, e_dev), F32)
        for f in range(FACES):
            hit = jnp.where((side[f : f + 1] == d) & (local[f : f + 1] == row), 1.0, hit)
        seen.append(jnp.max(hit, axis=1, keepdims=True))
    for f in range(FACES):
        there = jnp.zeros((e_dev, e_dev), F32)
        for d in range(4):
            there = jnp.where(side[f : f + 1] == d, seen[d], there)
        before = jnp.sum(jnp.where(row < local[f : f + 1], there, 0.0), axis=0, keepdims=True).astype(jnp.int32)
        halo = e_dev + HALO * side[f : f + 1] + jnp.minimum(before, HALO - 1)
        out_ref[f : f + 1, 0:e_dev] = jnp.where(side[f : f + 1] < 4, halo, local[f : f + 1]) + mode[f : f + 1]
    out_ref[FACES : FACES + 1, 0:e_dev] = slot
    lane = lax.broadcasted_iota(jnp.int32, (1, LANES), 1)
    rows = jnp.zeros((1, LANES), jnp.int32)
    for t in range(TOUCH):
        row = crow_ref[touch_ref[t, device]]
        owner = row // rows_own
        rows = jnp.where(lane == t, owner, jnp.where(lane == 8 + t, row - owner * rows_own + 1, rows))
    out_ref[FACES + 1 : FACES + 2] = rows
    p_copy.wait()

    def four(i, c):
        for j in range(4):
            fetch(4 * i + j).wait()
        for j in range(4):
            e = 4 * i + j
            for k in range(BLOCKS):
                lefts[e, k] = jnp.dot(pbuf[e], abuf[e, k], preferred_element_type=F32).astype(BF16)
        return c

    lax.fori_loop(0, early // 4, four, 0)


def main_kernel(route_hbm, a_hbm, p_hbm, done, h0, h1, h2, h3,
                out_ref, abuf, pool, acc, lefts0, lefts1, route_ref, a_sems, h_sems):
    e_dev, width_c, _ = p_hbm.shape
    early = done.shape[0]

    def fetch(e):
        return pltpu.make_async_copy(a_hbm.at[e], abuf.at[e - early], a_sems.at[e - early])

    own_copy = pltpu.make_async_copy(p_hbm, pool.at[pl.ds(0, e_dev)], h_sems.at[4])
    own_copy.start()
    route_copy = pltpu.make_async_copy(route_hbm, route_ref, h_sems.at[5])
    route_copy.start()
    halos = [
        pltpu.make_async_copy(h.at[pl.ds(0, HALO)], pool.at[pl.ds(e_dev + HALO * d, HALO)], h_sems.at[d])
        for d, h in enumerate((h0, h1, h2, h3))
    ]
    for copy in halos:
        copy.start()
    for e in range(early, early + WINDOW):
        fetch(e).start()
    acc[...] = jnp.zeros_like(acc)
    out_ref[...] = jnp.zeros_like(out_ref)
    own_copy.wait()
    route_copy.wait()
    for copy in halos:
        copy.wait()

    def make_lefts(e, lefts):
        left = pool[e]
        for k in range(BLOCKS):
            lefts[k] = jnp.dot(left, abuf[e - early, k], preferred_element_type=F32).astype(BF16)

    def add_products(e, lefts):
        slot = route_ref[FACES, e]
        total = None
        for k in range(BLOCKS):
            if k == 0:
                right = pool[e]
            else:
                route = route_ref[k - 1, e]
                right = pool[route & (SAME - 1)]
            prod = lax.dot_general(lefts[k], right, (((1,), (1,)), ((), ())), preferred_element_type=F32)
            if k == 0:
                total = prod
                continue
            total = total + jnp.where((route & SAME) != 0, prod, 0.0)
            at = pl.multiple_of((slot * 8 + k) * width_c, width_c)
            acc[pl.ds(at, width_c), 0:width_c] += jnp.where((route & APART) != 0, prod, 0.0)
        at = pl.multiple_of(slot * 8 * width_c, width_c)
        acc[pl.ds(at, width_c), 0:width_c] += total

    def ready(i, c):
        for j in range(4):
            add_products(4 * i + j, done.at[4 * i + j])
        return c

    lax.fori_loop(0, early // 4, ready, 0)
    fetch(early).wait()
    make_lefts(early, lefts0)

    def two(i, c):
        e = early + 2 * i + 1
        for ahead in range(2):

            @pl.when(e + ahead + WINDOW - 1 < e_dev)
            def _():
                fetch(e + ahead + WINDOW - 1).start()

        fetch(e).wait()
        fetch(e + 1).wait()
        add_products(e - 1, lefts0)
        make_lefts(e, lefts1)
        add_products(e, lefts1)
        make_lefts(e + 1, lefts0)
        return c

    lax.fori_loop(0, (e_dev - early) // 2 - 1, two, 0)
    fetch(e_dev - 1).wait()
    make_lefts(e_dev - 1, lefts1)
    add_products(e_dev - 2, lefts0)
    add_products(e_dev - 1, lefts1)

    lane = lax.broadcasted_iota(jnp.int32, (8, LANES), 1)
    sub = lax.broadcasted_iota(jnp.int32, (8, LANES), 0)
    per = LANES // width_c
    for t in range(TOUCH):
        owner = route_ref[FACES + 1, t]
        code = route_ref[FACES + 1, 8 + t].astype(F32)
        for j in range(width_c // per):
            value = None
            for i in range(per):
                piece = acc[pl.ds(t * 8 * width_c + j * per + i, 8, stride=width_c), :]
                if i == 0:
                    value = piece
                else:
                    piece = pltpu.roll(piece, i * width_c, 1)
                    value = jnp.where(lane >= i * width_c, piece, value)
            value = jnp.where(sub == 7, code, value)
            out_ref[owner, :, j * LANES : (j + 1) * LANES] = value.astype(BF16)


def combine_kernel(rows_own, group_rows, in_ref, out_ref, rank, codes):
    slots, width = in_ref.shape
    n_dev = slots // 8
    piece = out_ref.shape[0]

    def clear(i, c):
        rank[i] = -1
        return c

    lax.fori_loop(0, rows_own + 1, clear, 0, unroll=8)
    for r in range(group_rows + 1):
        codes[r] = 0
    used = jnp.int32(0)
    lane = lax.broadcasted_iota(jnp.int32, (1, slots), 1)
    key = jnp.full((1, slots), -1, jnp.int32)
    for d in range(n_dev):
        code = in_ref[8 * d : 8 * d + 8, 0:LANES].astype(F32)[7, 0].astype(jnp.int32)
        old = rank[code]
        fresh = (code > 0) & (old < 0)
        at = jnp.where(code > 0, jnp.where(old < 0, jnp.minimum(used, group_rows - 1), old), group_rows)
        rank[code] = jnp.where(code > 0, at, -1)
        codes[at] = code
        used = used + fresh.astype(jnp.int32)
        mine = (lane >= 8 * d) & (lane < 8 * d + 7)
        key = jnp.where(mine, jnp.where(code > 0, (lane - 8 * d) * group_rows + at, -1), key)
    row = lax.broadcasted_iota(jnp.int32, (piece, slots), 0)
    chosen = jnp.where(row == key, 1.0, 0.0).astype(BF16)
    out = jnp.dot(chosen, in_ref[...], preferred_element_type=F32)
    at = lax.broadcasted_iota(jnp.int32, (1, width), 1) % piece
    of_row = at % group_rows
    tags = jnp.zeros((1, width), F32)
    for r in range(group_rows):
        tags = jnp.where((of_row == r) & (at < BLOCKS * group_rows), codes[r].astype(F32), tags)
    rows = lax.broadcasted_iota(jnp.int32, (piece, width), 0)
    out_ref[...] = jnp.where(rows >= BLOCKS * group_rows, tags, out).astype(BF16)


def scatter_kernel(rows_own, group_rows, *refs):
    ins, out_hbm, held, chosen, out_buf, out_sems = refs[:-5], *refs[-5:]
    width = out_buf.shape[1]
    piece = ins[0].shape[0]
    depth = held.shape[0]
    for q, ref in enumerate(ins):
        held[q * piece : (q + 1) * piece] = ref[...]
    lane = lax.broadcasted_iota(jnp.int32, (1, depth), 1)
    in_piece = lane % piece
    block = in_piece // group_rows
    tags = jnp.zeros((1, depth), F32)
    for q, ref in enumerate(ins):
        tag = ref[piece - 8 : piece, 0:depth].astype(F32)[7:8]
        tags = jnp.where((lane >= q * piece) & (lane < (q + 1) * piece), tag, tags)
    tags = tags.astype(jnp.int32)
    key = jnp.where((tags > 0) & (block < BLOCKS), block * rows_own + tags - 1, -1)
    for s in range(BLOCKS):
        row = lax.broadcasted_iota(jnp.int32, (rows_own, depth), 0) + s * rows_own
        chosen[s * rows_own : (s + 1) * rows_own] = jnp.where(row == key, 1.0, 0.0).astype(BF16)
    n_out = out_sems.shape[0]
    step = width // n_out
    outs = []
    for n in range(n_out):
        cols = pl.ds(n * step, step)
        out_buf[:, n * step : (n + 1) * step] = jnp.dot(
            chosen[...], held[:, n * step : (n + 1) * step], preferred_element_type=F32
        )
        copy = pltpu.make_async_copy(out_buf.at[:, cols], out_hbm.at[:, cols], out_sems.at[n])
        copy.start()
        outs.append(copy)
    for copy in outs:
        copy.wait()


def on_device(a_blocks, prolong_t, elem_slot, touch_agg, nbr, nbr_agg, coarse_row):
    n_grp = lax.axis_size("grp")
    n_dev = lax.axis_size("dev")
    e_dev, width_c, width_b = prolong_t.shape
    half = 2
    group_rows = ((n_dev * half + 1) + half) // (half + 1)
    rows_own = n_grp * group_rows
    width = width_c * width_c
    pin = lambda x: pltpu.with_memory_space_constraint(x, pltpu.MemorySpace.HBM)
    smem = pl.BlockSpec(memory_space=SMEM)
    vmem = pl.BlockSpec(memory_space=VMEM)
    hbm = pl.BlockSpec(memory_space=pl.ANY)

    def params(mib):
        return pltpu.CompilerParams(vmem_limit_bytes=mib << 20)

    def pack(*args):
        return pack_kernel(n_dev, *args)

    halo_shape = jax.ShapeDtypeStruct((HALO + 1, width_c, width_b), BF16)
    packed = pl.pallas_call(
        pack, out_shape=(halo_shape,) * 4, in_specs=[hbm] * 2, out_specs=(vmem,) * 4,
        scratch_shapes=[pltpu.SMEM((FACES, e_dev), jnp.int32), pltpu.VMEM((e_dev, width_c, width_b), BF16),
                        pltpu.SemaphoreType.DMA((5,))],
        compiler_params=params(8), name="pack",
    )(pin(nbr.T), pin(prolong_t))
    up = lambda size: [(i, (i + 1) % size) for i in range(size)]
    down = lambda size: [((i + 1) % size, i) for i in range(size)]
    from_low = lax.ppermute(packed[1], "grp", up(n_grp))
    from_high = lax.ppermute(packed[0], "grp", down(n_grp))
    from_left = lax.ppermute(packed[3], "dev", up(n_dev))
    from_right = lax.ppermute(packed[2], "dev", down(n_dev))

    def early(*args):
        return early_kernel(n_dev, rows_own, *args)

    routes, lefts = pl.pallas_call(
        early,
        out_shape=(jax.ShapeDtypeStruct((8, LANES), jnp.int32), jax.ShapeDtypeStruct((EARLY, BLOCKS, width_c, width_b), BF16)),
        in_specs=[hbm] * 7, out_specs=(vmem, vmem),
        scratch_shapes=[
            pltpu.VMEM((EARLY, BLOCKS, width_b, width_b), BF16),
            pltpu.VMEM((EARLY, width_c, width_b), BF16),
            pltpu.VMEM((1, e_dev), jnp.int32),
            pltpu.VMEM((FACES, e_dev), jnp.int32),
            pltpu.VMEM((FACES, e_dev), jnp.int32),
            pltpu.SMEM(touch_agg.T.shape, jnp.int32),
            pltpu.SMEM(coarse_row.shape, jnp.int32),
            pltpu.SemaphoreType.DMA((EARLY,)),
            pltpu.SemaphoreType.DMA(()),
            pltpu.SemaphoreType.DMA((5,)),
        ],
        compiler_params=params(18), name="early",
    )(*map(pin, (elem_slot.reshape(1, e_dev), nbr.T, nbr_agg.T, touch_agg.T, coarse_row, a_blocks, prolong_t)))

    outgoing = pl.pallas_call(
        main_kernel, out_shape=jax.ShapeDtypeStruct((n_dev, 8, width), BF16),
        in_specs=[hbm] * 3 + [vmem] + [hbm] * 4, out_specs=vmem,
        scratch_shapes=[
            pltpu.VMEM((e_dev - EARLY, BLOCKS, width_b, width_b), BF16),
            pltpu.VMEM((e_dev + 4 * HALO, width_c, width_b), BF16),
            pltpu.VMEM((TOUCH * 8 * width_c, LANES), F32),
            pltpu.VMEM((BLOCKS, width_c, width_b), BF16),
            pltpu.VMEM((BLOCKS, width_c, width_b), BF16),
            pltpu.SMEM((8, LANES), jnp.int32),
            pltpu.SemaphoreType.DMA((e_dev - EARLY,)),
            pltpu.SemaphoreType.DMA((6,)),
        ],
        compiler_params=params(36), name="products",
    )(routes, pin(a_blocks), prolong_t, lefts, from_low, from_high, from_left, from_right)
    incoming = lax.all_to_all(outgoing, "dev", split_axis=0, concat_axis=0, tiled=True)
    piece = 8 * ((BLOCKS * group_rows) // 8 + 1)

    def combine(*args):
        return combine_kernel(rows_own, group_rows, *args)

    mine = pl.pallas_call(
        combine, out_shape=jax.ShapeDtypeStruct((piece, width), BF16), in_specs=[vmem], out_specs=vmem,
        scratch_shapes=[pltpu.SMEM((rows_own + 1,), jnp.int32), pltpu.SMEM((group_rows + 1,), jnp.int32)],
        compiler_params=params(8), name="combine",
    )(incoming.reshape(n_dev * 8, width))
    swap = [(i, i ^ 1) for i in range(n_grp)]
    across = [lax.ppermute(mine, "grp", [(i, (i + 2 * k) % n_grp) for i in range(n_grp)]) for k in range(1, n_grp // 2)]
    twin = lax.ppermute(mine, "grp", swap)
    others = [lax.ppermute(part, "grp", swap) for part in across]
    pieces = (mine, twin, *across, *others)

    def scatter(*args):
        return scatter_kernel(rows_own, group_rows, *args)

    out = pl.pallas_call(
        scatter, out_shape=jax.ShapeDtypeStruct((BLOCKS * rows_own, width), F32), in_specs=[vmem] * len(pieces),
        out_specs=hbm,
        scratch_shapes=[
            pltpu.VMEM((n_grp * piece, width), BF16),
            pltpu.VMEM((BLOCKS * rows_own, n_grp * piece), BF16),
            pltpu.VMEM((BLOCKS * rows_own, width), F32),
            pltpu.SemaphoreType.DMA((4,)),
        ],
        compiler_params=params(16), name="scatter",
    )(*pieces)
    return jnp.swapaxes(out.reshape(BLOCKS, rows_own, width), 0, 1)


def solution(mesh):
    in_specs = (
        P(("grp", "dev"), None, None, None),
        P(("grp", "dev"), None, None),
        P(("grp", "dev")),
        P(),
        P(("grp", "dev"), None),
        P(("grp", "dev"), None),
        P(),
    )
    return jax.shard_map(
        on_device, mesh=mesh, in_specs=in_specs, out_specs=P("dev", None, None), check_vma=False
    )
```

```python
import jax
import jax.numpy as jnp
from jax import lax
from jax.experimental import pallas as pl
from jax.experimental.pallas import tpu as pltpu
from jax.sharding import PartitionSpec as P

TOUCH = 6
FACES = 6
BLOCKS = 7
LANES = 128
HALO = 8
WINDOW = 8
EARLY = 20
SAME = 256
APART = 512
F32 = jnp.float32
BF16 = jnp.bfloat16
SMEM = pltpu.MemorySpace.SMEM
VMEM = pltpu.MemorySpace.VMEM


def position(n_dev):
    return lax.axis_index("grp") * n_dev + lax.axis_index("dev")


def load(pairs):
    copies = [pltpu.make_async_copy(src, dst, sem) for src, dst, sem in pairs]
    for copy in copies:
        copy.start()
    return copies


def pack_kernel(n_dev, nbr_hbm, p_hbm, *refs):
    outs, nbr_ref, p_ref, sems = refs[:4], *refs[4:]
    e_dev = p_ref.shape[0]
    quarter = e_dev // 4
    copies = load(
        [(nbr_hbm, nbr_ref, sems.at[4])]
        + [(p_hbm.at[pl.ds(i * quarter, quarter)], p_ref.at[pl.ds(i * quarter, quarter)], sems.at[i]) for i in range(4)]
    )
    for copy in copies:
        copy.wait()
    shift = e_dev.bit_length() - 1
    device = position(n_dev)
    homes = (device - n_dev, device + n_dev, device - 1, device + 1)

    def step(e, counts):
        hits = [jnp.bool_(False)] * 4
        for f in range(FACES):
            home = lax.shift_right_arithmetic(nbr_ref[f, e], shift)
            hits = [hit | (home == h) for hit, h in zip(hits, homes)]
        block = p_ref[e]
        new = []
        for d in range(4):
            outs[d][jnp.minimum(counts[d], HALO)] = block
            new.append(counts[d] + hits[d].astype(jnp.int32))
        return tuple(new)

    lax.fori_loop(0, e_dev, step, (jnp.int32(0),) * 4, unroll=16)


def early_kernel(n_dev, rows_own, slot_hbm, nbr_hbm, nagg_hbm, touch_hbm, crow_hbm, a_hbm, p_hbm, out_ref, lefts,
                 abuf, pbuf, slot_ref, nbr_ref, nagg_ref, touch_ref, crow_ref, a_sems, p_sem, sems):
    early = lefts.shape[0]
    small = load(
        [
            (slot_hbm, slot_ref, sems.at[0]),
            (nbr_hbm, nbr_ref, sems.at[1]),
            (nagg_hbm, nagg_ref, sems.at[2]),
            (touch_hbm, touch_ref, sems.at[3]),
            (crow_hbm, crow_ref, sems.at[4]),
        ]
    )

    def fetch(e):
        return pltpu.make_async_copy(a_hbm.at[e], abuf.at[e], a_sems.at[e])

    p_copy = pltpu.make_async_copy(p_hbm.at[pl.ds(0, early)], pbuf, p_sem)
    for e in range(early):
        fetch(e).start()
    p_copy.start()
    e_dev = slot_ref.shape[1]
    shift = e_dev.bit_length() - 1
    device = position(n_dev)
    for copy in small:
        copy.wait()
    nbr = nbr_ref[...]
    home = lax.shift_right_arithmetic(nbr, shift)
    local = nbr & (e_dev - 1)
    side = jnp.full(nbr.shape, 4, jnp.int32)
    for d, h in enumerate((device - n_dev, device + n_dev, device - 1, device + 1)):
        side = jnp.where(home == h, d, side)
    slot = slot_ref[...]
    own = jnp.zeros_like(slot)
    for t in range(TOUCH):
        own = jnp.where(slot == t, touch_ref[t, device], own)
    mode = jnp.where(nbr < 0, 0, jnp.where(nagg_ref[...] == own, SAME, APART))
    row = lax.broadcasted_iota(jnp.int32, (e_dev, e_dev), 0)
    seen = []
    for d in range(4):
        hit = jnp.zeros((e_dev, e_dev), F32)
        for f in range(FACES):
            hit = jnp.where((side[f : f + 1] == d) & (local[f : f + 1] == row), 1.0, hit)
        seen.append(jnp.max(hit, axis=1, keepdims=True))
    for f in range(FACES):
        there = jnp.zeros((e_dev, e_dev), F32)
        for d in range(4):
            there = jnp.where(side[f : f + 1] == d, seen[d], there)
        before = jnp.sum(jnp.where(row < local[f : f + 1], there, 0.0), axis=0, keepdims=True).astype(jnp.int32)
        halo = e_dev + HALO * side[f : f + 1] + jnp.minimum(before, HALO - 1)
        out_ref[f : f + 1, 0:e_dev] = jnp.where(side[f : f + 1] < 4, halo, local[f : f + 1]) + mode[f : f + 1]
    out_ref[FACES : FACES + 1, 0:e_dev] = slot
    lane = lax.broadcasted_iota(jnp.int32, (1, LANES), 1)
    rows = jnp.zeros((1, LANES), jnp.int32)
    for t in range(TOUCH):
        row = crow_ref[touch_ref[t, device]]
        owner = row // rows_own
        rows = jnp.where(lane == t, owner, jnp.where(lane == 8 + t, row - owner * rows_own + 1, rows))
    out_ref[FACES + 1 : FACES + 2] = rows
    p_copy.wait()

    def four(i, c):
        for j in range(4):
            fetch(4 * i + j).wait()
        for j in range(4):
            e = 4 * i + j
            for k in range(BLOCKS):
                lefts[e, k] = jnp.dot(pbuf[e], abuf[e, k], preferred_element_type=F32).astype(BF16)
        return c

    lax.fori_loop(0, early // 4, four, 0)


def main_kernel(route_hbm, a_hbm, p_hbm, done, h0, h1, h2, h3,
                out_ref, abuf, pool, acc, lefts0, lefts1, route_ref, a_sems, h_sems):
    e_dev, width_c, _ = p_hbm.shape
    early = done.shape[0]

    def fetch(e):
        return pltpu.make_async_copy(a_hbm.at[e], abuf.at[e - early], a_sems.at[e - early])

    own_copy = pltpu.make_async_copy(p_hbm, pool.at[pl.ds(0, e_dev)], h_sems.at[4])
    own_copy.start()
    route_copy = pltpu.make_async_copy(route_hbm, route_ref, h_sems.at[5])
    route_copy.start()
    halos = [
        pltpu.make_async_copy(h.at[pl.ds(0, HALO)], pool.at[pl.ds(e_dev + HALO * d, HALO)], h_sems.at[d])
        for d, h in enumerate((h0, h1, h2, h3))
    ]
    for copy in halos:
        copy.start()
    for e in range(early, early + WINDOW):
        fetch(e).start()
    acc[...] = jnp.zeros_like(acc)
    out_ref[...] = jnp.zeros_like(out_ref)
    own_copy.wait()
    route_copy.wait()
    for copy in halos:
        copy.wait()

    def make_lefts(e, lefts):
        left = pool[e]
        for k in range(BLOCKS):
            lefts[k] = jnp.dot(left, abuf[e - early, k], preferred_element_type=F32).astype(BF16)

    def add_products(e, lefts):
        slot = route_ref[FACES, e]
        total = None
        for k in range(BLOCKS):
            if k == 0:
                right = pool[e]
            else:
                route = route_ref[k - 1, e]
                right = pool[route & (SAME - 1)]
            prod = lax.dot_general(lefts[k], right, (((1,), (1,)), ((), ())), preferred_element_type=F32)
            if k == 0:
                total = prod
                continue
            total = total + jnp.where((route & SAME) != 0, prod, 0.0)
            at = pl.multiple_of((slot * 8 + k) * width_c, width_c)
            acc[pl.ds(at, width_c), 0:width_c] += jnp.where((route & APART) != 0, prod, 0.0)
        at = pl.multiple_of(slot * 8 * width_c, width_c)
        acc[pl.ds(at, width_c), 0:width_c] += total

    def ready(i, c):
        for j in range(4):
            add_products(4 * i + j, done.at[4 * i + j])
        return c

    lax.fori_loop(0, early // 4, ready, 0)
    fetch(early).wait()
    make_lefts(early, lefts0)

    def two(i, c):
        e = early + 2 * i + 1
        for ahead in range(2):

            @pl.when(e + ahead + WINDOW - 1 < e_dev)
            def _():
                fetch(e + ahead + WINDOW - 1).start()

        fetch(e).wait()
        fetch(e + 1).wait()
        add_products(e - 1, lefts0)
        make_lefts(e, lefts1)
        add_products(e, lefts1)
        make_lefts(e + 1, lefts0)
        return c

    lax.fori_loop(0, (e_dev - early) // 2 - 1, two, 0)
    fetch(e_dev - 1).wait()
    make_lefts(e_dev - 1, lefts1)
    add_products(e_dev - 2, lefts0)
    add_products(e_dev - 1, lefts1)

    lane = lax.broadcasted_iota(jnp.int32, (8, LANES), 1)
    sub = lax.broadcasted_iota(jnp.int32, (8, LANES), 0)
    per = LANES // width_c
    for t in range(TOUCH):
        owner = route_ref[FACES + 1, t]
        code = route_ref[FACES + 1, 8 + t].astype(F32)
        for j in range(width_c // per):
            value = None
            for i in range(per):
                piece = acc[pl.ds(t * 8 * width_c + j * per + i, 8, stride=width_c), :]
                if i == 0:
                    value = piece
                else:
                    piece = pltpu.roll(piece, i * width_c, 1)
                    value = jnp.where(lane >= i * width_c, piece, value)
            value = jnp.where(sub == 7, code, value)
            out_ref[owner, :, j * LANES : (j + 1) * LANES] = value.astype(BF16)


def combine_kernel(rows_own, group_rows, in_ref, out_ref, rank, codes):
    slots, width = in_ref.shape
    n_dev = slots // 8
    piece = out_ref.shape[0]

    def clear(i, c):
        rank[i] = -1
        return c

    lax.fori_loop(0, rows_own + 1, clear, 0, unroll=8)
    for r in range(group_rows + 1):
        codes[r] = 0
    used = jnp.int32(0)
    lane = lax.broadcasted_iota(jnp.int32, (1, slots), 1)
    key = jnp.full((1, slots), -1, jnp.int32)
    for d in range(n_dev):
        code = in_ref[8 * d : 8 * d + 8, 0:LANES].astype(F32)[7, 0].astype(jnp.int32)
        old = rank[code]
        fresh = (code > 0) & (old < 0)
        at = jnp.where(code > 0, jnp.where(old < 0, jnp.minimum(used, group_rows - 1), old), group_rows)
        rank[code] = jnp.where(code > 0, at, -1)
        codes[at] = code
        used = used + fresh.astype(jnp.int32)
        mine = (lane >= 8 * d) & (lane < 8 * d + 7)
        key = jnp.where(mine, jnp.where(code > 0, (lane - 8 * d) * group_rows + at, -1), key)
    row = lax.broadcasted_iota(jnp.int32, (piece, slots), 0)
    chosen = jnp.where(row == key, 1.0, 0.0).astype(BF16)
    out = jnp.dot(chosen, in_ref[...], preferred_element_type=F32)
    at = lax.broadcasted_iota(jnp.int32, (1, width), 1) % piece
    of_row = at % group_rows
    tags = jnp.zeros((1, width), F32)
    for r in range(group_rows):
        tags = jnp.where((of_row == r) & (at < BLOCKS * group_rows), codes[r].astype(F32), tags)
    rows = lax.broadcasted_iota(jnp.int32, (piece, width), 0)
    out_ref[...] = jnp.where(rows >= BLOCKS * group_rows, tags, out).astype(BF16)


def scatter_kernel(rows_own, group_rows, *refs):
    ins, out_hbm, held, chosen, out_buf, out_sems = refs[:-5], *refs[-5:]
    width = out_buf.shape[1]
    piece = ins[0].shape[0]
    depth = held.shape[0]
    for q, ref in enumerate(ins):
        held[q * piece : (q + 1) * piece] = ref[...]
    lane = lax.broadcasted_iota(jnp.int32, (1, depth), 1)
    in_piece = lane % piece
    block = in_piece // group_rows
    tags = jnp.zeros((1, depth), F32)
    for q, ref in enumerate(ins):
        tag = ref[piece - 8 : piece, 0:depth].astype(F32)[7:8]
        tags = jnp.where((lane >= q * piece) & (lane < (q + 1) * piece), tag, tags)
    tags = tags.astype(jnp.int32)
    key = jnp.where((tags > 0) & (block < BLOCKS), block * rows_own + tags - 1, -1)
    for s in range(BLOCKS):
        row = lax.broadcasted_iota(jnp.int32, (rows_own, depth), 0) + s * rows_own
        chosen[s * rows_own : (s + 1) * rows_own] = jnp.where(row == key, 1.0, 0.0).astype(BF16)
    n_out = out_sems.shape[0]
    step = width // n_out
    outs = []
    for n in range(n_out):
        cols = pl.ds(n * step, step)
        out_buf[:, n * step : (n + 1) * step] = jnp.dot(
            chosen[...], held[:, n * step : (n + 1) * step], preferred_element_type=F32
        )
        copy = pltpu.make_async_copy(out_buf.at[:, cols], out_hbm.at[:, cols], out_sems.at[n])
        copy.start()
        outs.append(copy)
    for copy in outs:
        copy.wait()


def on_device(a_blocks, prolong_t, elem_slot, touch_agg, nbr, nbr_agg, coarse_row):
    n_grp = lax.axis_size("grp")
    n_dev = lax.axis_size("dev")
    e_dev, width_c, width_b = prolong_t.shape
    half = 2
    group_rows = ((n_dev * half + 1) + half) // (half + 1)
    rows_own = n_grp * group_rows
    width = width_c * width_c
    pin = lambda x: pltpu.with_memory_space_constraint(x, pltpu.MemorySpace.HBM)
    smem = pl.BlockSpec(memory_space=SMEM)
    vmem = pl.BlockSpec(memory_space=VMEM)
    hbm = pl.BlockSpec(memory_space=pl.ANY)

    def params(mib):
        return pltpu.CompilerParams(vmem_limit_bytes=mib << 20)

    def pack(*args):
        return pack_kernel(n_dev, *args)

    halo_shape = jax.ShapeDtypeStruct((HALO + 1, width_c, width_b), BF16)
    packed = pl.pallas_call(
        pack, out_shape=(halo_shape,) * 4, in_specs=[hbm] * 2, out_specs=(vmem,) * 4,
        scratch_shapes=[pltpu.SMEM((FACES, e_dev), jnp.int32), pltpu.VMEM((e_dev, width_c, width_b), BF16),
                        pltpu.SemaphoreType.DMA((5,))],
        compiler_params=params(8), name="pack",
    )(pin(nbr.T), pin(prolong_t))
    up = lambda size: [(i, (i + 1) % size) for i in range(size)]
    down = lambda size: [((i + 1) % size, i) for i in range(size)]
    from_low = lax.ppermute(packed[1], "grp", up(n_grp))
    from_high = lax.ppermute(packed[0], "grp", down(n_grp))
    from_left = lax.ppermute(packed[3], "dev", up(n_dev))
    from_right = lax.ppermute(packed[2], "dev", down(n_dev))

    def early(*args):
        return early_kernel(n_dev, rows_own, *args)

    routes, lefts = pl.pallas_call(
        early,
        out_shape=(jax.ShapeDtypeStruct((8, LANES), jnp.int32), jax.ShapeDtypeStruct((EARLY, BLOCKS, width_c, width_b), BF16)),
        in_specs=[hbm] * 7, out_specs=(vmem, vmem),
        scratch_shapes=[
            pltpu.VMEM((EARLY, BLOCKS, width_b, width_b), BF16),
            pltpu.VMEM((EARLY, width_c, width_b), BF16),
            pltpu.VMEM((1, e_dev), jnp.int32),
            pltpu.VMEM((FACES, e_dev), jnp.int32),
            pltpu.VMEM((FACES, e_dev), jnp.int32),
            pltpu.SMEM(touch_agg.T.shape, jnp.int32),
            pltpu.SMEM(coarse_row.shape, jnp.int32),
            pltpu.SemaphoreType.DMA((EARLY,)),
            pltpu.SemaphoreType.DMA(()),
            pltpu.SemaphoreType.DMA((5,)),
        ],
        compiler_params=params(24), name="early",
    )(*map(pin, (elem_slot.reshape(1, e_dev), nbr.T, nbr_agg.T, touch_agg.T, coarse_row, a_blocks, prolong_t)))

    outgoing = pl.pallas_call(
        main_kernel, out_shape=jax.ShapeDtypeStruct((n_dev, 8, width), BF16),
        in_specs=[hbm] * 3 + [vmem] + [hbm] * 4, out_specs=vmem,
        scratch_shapes=[
            pltpu.VMEM((e_dev - EARLY, BLOCKS, width_b, width_b), BF16),
            pltpu.VMEM((e_dev + 4 * HALO, width_c, width_b), BF16),
            pltpu.VMEM((TOUCH * 8 * width_c, LANES), F32),
            pltpu.VMEM((BLOCKS, width_c, width_b), BF16),
            pltpu.VMEM((BLOCKS, width_c, width_b), BF16),
            pltpu.SMEM((8, LANES), jnp.int32),
            pltpu.SemaphoreType.DMA((e_dev - EARLY,)),
            pltpu.SemaphoreType.DMA((6,)),
        ],
        compiler_params=params(36), name="products",
    )(routes, pin(a_blocks), prolong_t, lefts, from_low, from_high, from_left, from_right)
    incoming = lax.all_to_all(outgoing, "dev", split_axis=0, concat_axis=0, tiled=True)
    piece = 8 * ((BLOCKS * group_rows) // 8 + 1)

    def combine(*args):
        return combine_kernel(rows_own, group_rows, *args)

    mine = pl.pallas_call(
        combine, out_shape=jax.ShapeDtypeStruct((piece, width), BF16), in_specs=[vmem], out_specs=vmem,
        scratch_shapes=[pltpu.SMEM((rows_own + 1,), jnp.int32), pltpu.SMEM((group_rows + 1,), jnp.int32)],
        compiler_params=params(8), name="combine",
    )(incoming.reshape(n_dev * 8, width))
    swap = [(i, i ^ 1) for i in range(n_grp)]
    across = [lax.ppermute(mine, "grp", [(i, (i + 2 * k) % n_grp) for i in range(n_grp)]) for k in range(1, n_grp // 2)]
    twin = lax.ppermute(mine, "grp", swap)
    others = [lax.ppermute(part, "grp", swap) for part in across]
    pieces = (mine, twin, *across, *others)

    def scatter(*args):
        return scatter_kernel(rows_own, group_rows, *args)

    out = pl.pallas_call(
        scatter, out_shape=jax.ShapeDtypeStruct((BLOCKS * rows_own, width), F32), in_specs=[vmem] * len(pieces),
        out_specs=hbm,
        scratch_shapes=[
            pltpu.VMEM((n_grp * piece, width), BF16),
            pltpu.VMEM((BLOCKS * rows_own, n_grp * piece), BF16),
            pltpu.VMEM((BLOCKS * rows_own, width), F32),
            pltpu.SemaphoreType.DMA((2,)),
        ],
        compiler_params=params(16), name="scatter",
    )(*pieces)
    return jnp.swapaxes(out.reshape(BLOCKS, rows_own, width), 0, 1)


def solution(mesh):
    in_specs = (
        P(("grp", "dev"), None, None, None),
        P(("grp", "dev"), None, None),
        P(("grp", "dev")),
        P(),
        P(("grp", "dev"), None),
        P(("grp", "dev"), None),
        P(),
    )
    return jax.shard_map(
        on_device, mesh=mesh, in_specs=in_specs, out_specs=P("dev", None, None), check_vma=False
    )
```
